256 devices in a mesh: space: 64 (over x, y, z_hi), chan: 4 (over z_lo, core).
Axes of the slice: x: 4, y: 4, z: 8 (z_hi: 4, z_lo: 2; z = z_hi * 2 + z_lo), core: 2. Of those that a mesh axis runs over, the one named last changes fastest.
Arguments:
- features: bfloat16 [64, 128, 8, 8, 256], P('space'), may hold values from -6 to 6
- column_heights: int32 [64], replicated, may hold values from 1 to 32, as said below
- weight_one: bfloat16 [27, 128, 128], P(None, 'chan'), may hold values from -0.109375 to 0.109375
- bias_one: float32 [128], P('chan'), may hold values from 0 to 1
- weight_two: bfloat16 [27, 128, 128], P(None, 'chan'), may hold values from -0.109375 to 0.109375
- bias_two: float32 [128], P('chan'), may hold values from 0 to 1
Outputs:
- output: bfloat16 [64, 128, 8, 8, 256], P('space', 'chan')
The draws below stay inside these ranges and needn't reach their ends.
Inputs may be any that keep to these rules, and one draw needn't show every extreme that they name: Column c holds its active bricks at its lowest column_heights[c] of 32 levels; some column holds exactly 32.
All inputs are finite; a program needn't handle non-finite values.
Results may differ from the reference program's by a relative error of at most 0.004.
Values may be sent and summed in bfloat16 or wider, within the bound.
A program may use at most 128 MiB of HBM per device.

```python
import jax
import jax.numpy as jnp
from jax import lax

CHANNELS = 128
COL_Y = 8
BRICKS_Z = 32
COLUMNS = 64
DEPTH = 256


def draw_column_heights(key, part):
    key_levels, key_tallest = jax.random.split(key)
    levels = jax.random.randint(key_levels, (COLUMNS,), 0, BRICKS_Z)
    heights = 1 + levels * levels // BRICKS_Z
    tallest = jax.random.randint(key_tallest, (), 0, COLUMNS)
    return jnp.where(jnp.arange(COLUMNS) == tallest, BRICKS_Z, heights).astype(jnp.int32)


def block_scale(stream_key, extent, cuts, smallest, high):
    gain, own = 1.0, jax.random.fold_in(stream_key, 6)
    for dim, shards_of in cuts:
        steps = jnp.exp(jax.random.uniform(jax.random.fold_in(own, dim), (shards_of,), jnp.float32, smallest / len(cuts), high / len(cuts)))
        gain = gain * jnp.repeat(steps, extent[dim] // shards_of).reshape([-1 if axis == dim else 1 for axis in range(len(extent))])
    return gain


def bell_draw(own_key, dims, width, bound, cuts=(), kind=jnp.bfloat16):
    values = width * jax.random.normal(own_key, dims, jnp.float32)
    if cuts:
        values = values * block_scale(own_key, dims, cuts, -0.22, 0.18)
    return jnp.clip(values, -bound, bound).astype(kind)


def setup_inputs(seed: int = 0) -> dict:
    key_of = jax.random.split(jax.random.key(seed), 7)
    return {
        "features": bell_draw(key_of[0], (COLUMNS, CHANNELS, 8, 8, DEPTH), 1.0, 6.0, ((0, 64),)),
        "column_heights": draw_column_heights(jax.random.fold_in(key_of[6], 71), 0),
        "weight_one": bell_draw(key_of[2], (27, CHANNELS, CHANNELS), (27 * CHANNELS) ** -0.5, 0.109375, ((1, 4),)),
        "bias_one": jnp.clip(1.0 * jax.random.uniform(key_of[3], (CHANNELS,), jnp.float32) ** block_scale(key_of[3], (CHANNELS,), ((0, 4),), -0.2, 0.2), 0.0, 1.0),
        "weight_two": bell_draw(key_of[4], (27, CHANNELS, CHANNELS), (27 * CHANNELS) ** -0.5, 0.109375, ((1, 4),)),
        "bias_two": jnp.clip(1.0 * jax.random.uniform(key_of[5], (CHANNELS,), jnp.float32) ** block_scale(key_of[5], (CHANNELS,), ((0, 4),), -0.2, 0.2), 0.0, 1.0),
    }


def block_size(depth_cells):
    return 16


def conv_layer(columns_in, heights, weights, biases):
    grid_rows = COLUMNS // COL_Y
    volume = columns_in.reshape(grid_rows, COL_Y, CHANNELS, 8, 8, DEPTH)
    volume = volume.transpose(2, 0, 3, 1, 4, 5).reshape(CHANNELS, grid_rows * 8, COL_Y * 8, DEPTH)
    padded = jnp.pad(volume, ((0, 0), (1, 1), (1, 1), (1, 1)))
    block_len = block_size(DEPTH)
    weights_wide = weights.astype(jnp.float32)

    def column(col_id):
        grid_x = col_id // COL_Y
        grid_y = col_id % COL_Y
        anchor = jnp.zeros((), jnp.int32)
        box_part = lax.dynamic_slice(padded, (anchor, (grid_x * 8).astype(jnp.int32), (grid_y * 8).astype(jnp.int32), anchor), (CHANNELS, 10, 10, DEPTH + 2))
        live_top = (heights[col_id] * 8).astype(jnp.int32)
        blocks = (live_top + block_len - 1) // block_len

        def advance(block_id, output):
            start = (block_id * block_len).astype(jnp.int32)
            summed = jnp.zeros((CHANNELS, 64 * block_len), jnp.float32)
            for shift_x in range(3):
                for shift_y in range(3):
                    for shift_z in range(3):
                        sliced = lax.dynamic_slice(box_part, (anchor, anchor + shift_x, anchor + shift_y, start + shift_z), (CHANNELS, 8, 8, block_len))
                        sliced = sliced.reshape(CHANNELS, 64 * block_len).astype(jnp.float32)
                        summed = summed + jnp.dot(weights_wide[9 * shift_x + 3 * shift_y + shift_z], sliced, precision=lax.Precision.HIGHEST, preferred_element_type=jnp.float32)
            result = jax.nn.relu(summed + biases[:, None]).reshape(CHANNELS, 8, 8, block_len)
            inside = (start + jnp.arange(block_len, dtype=jnp.int32)) < live_top
            result = (result * inside.astype(jnp.float32)).astype(jnp.bfloat16)
            return lax.dynamic_update_slice(output, result, (anchor, anchor, anchor, start))

        return lax.fori_loop(0, blocks, advance, jnp.zeros((CHANNELS, 8, 8, DEPTH), jnp.bfloat16))

    return lax.map(column, jnp.arange(COLUMNS, dtype=jnp.int32))


def reference(features, column_heights, weight_one, bias_one, weight_two, bias_two):
    z_cells = jnp.arange(DEPTH, dtype=jnp.int32)
    active = (z_cells[None, :] < column_heights[:, None] * 8).astype(jnp.float32)
    inputs = (features * active[:, None, None, None, :].astype(features.dtype)).astype(jnp.bfloat16)
    hidden = conv_layer(inputs, column_heights, weight_one, bias_one)
    return conv_layer(hidden, column_heights, weight_two, bias_two)
```

```python
import functools

import jax
import jax.numpy as jnp
from jax import lax
from jax.experimental import pallas as pl
from jax.experimental.pallas import tpu as pltpu
from jax.sharding import PartitionSpec as P

COL_Y = 8
MESH = pl.DeviceIdType.MESH
DIRECTIONS = [(dx, dy) for dx in (-1, 0, 1) for dy in (-1, 0, 1) if (dx, dy) != (0, 0)]


def kernel(
    grid_x,
    grid_y,
    feat,
    heights,
    w_one,
    w_two,
    b_one,
    b_two,
    out,
    xx,
    stage,
    wall,
    bme,
    ball,
    bias,
    obuf,
    feat_sem,
    wl_sem,
    w_send,
    w_recv,
    b_send,
    b_recv,
    f_send,
    f_recv,
    h_send,
    h_recv,
    o_send,
    o_recv,
    o_local,
):
    column = lax.axis_index("space")
    chan = lax.axis_index("chan")
    core = chan % 2
    half = chan // 2
    col_x = column // grid_y
    col_y = column % grid_y
    fine_x = 2 * col_x + core
    fine_y = 2 * col_y + half
    depth = xx.shape[-1]
    base_y = 4 * half

    def inside(dx, dy):
        fx, fy = fine_x + dx, fine_y + dy
        return (fx >= 0) & (fx < 2 * grid_x) & (fy >= 0) & (fy < 2 * grid_y)

    def device_at(dx, dy):
        fx, fy = fine_x + dx, fine_y + dy
        return ((fx // 2) * grid_y + fy // 2, (fy % 2) * 2 + fx % 2)

    out_x = 2 * core - 1
    out_y = 2 * half - 1
    siblings = [
        (column, half * 2 + 1 - core),
        (column, (1 - half) * 2 + core),
        (column, (1 - half) * 2 + 1 - core),
    ]

    def feature_load(xl):
        return pltpu.make_async_copy(
            feat.at[0, :, 3 * core + xl], stage.at[xl], feat_sem.at[xl]
        )

    for xl in range(5):
        feature_load(xl).start()
    weights = (w_one, w_two)
    for layer in range(2):
        pltpu.make_async_copy(
            weights[layer], wall.at[layer, chan], wl_sem.at[layer]
        ).start()

    barrier = pltpu.get_barrier_semaphore()
    for dx, dy in DIRECTIONS:

        @pl.when(inside(dx, dy))
        def _():
            pl.semaphore_signal(
                barrier, inc=1, device_id=device_at(dx, dy), device_id_type=MESH
            )

    bme[...] = jnp.zeros_like(bme)
    bme[0:1, 0:32] = b_one[...]
    bme[1:2, 0:32] = b_two[...]

    peers = sum(inside(dx, dy).astype(jnp.int32) for dx, dy in DIRECTIONS)
    pl.semaphore_wait(barrier, peers)

    def weight_send(layer, k):
        return pltpu.make_async_remote_copy(
            src_ref=weights[layer],
            dst_ref=wall.at[layer, chan],
            send_sem=w_send.at[layer, k],
            recv_sem=w_recv.at[layer, k],
            device_id=siblings[k],
            device_id_type=MESH,
        )

    def bias_send(k):
        return pltpu.make_async_remote_copy(
            src_ref=bme,
            dst_ref=ball.at[chan],
            send_sem=b_send.at[k],
            recv_sem=b_recv.at[k],
            device_id=siblings[k],
            device_id_type=MESH,
        )

    for k in range(3):
        weight_send(0, k).start()
        bias_send(k).start()
    ball[chan] = bme[...]

    has_x = (col_x + out_x >= 0) & (col_x + out_x < grid_x)
    has_y = (col_y + out_y >= 0) & (col_y + out_y < grid_y)
    live_top = heights[column] * 8
    lanes = lax.broadcasted_iota(jnp.int32, (1, 1, depth), 2)
    live_row = jnp.where(lanes < live_top, 1.0, 0.0).astype(jnp.bfloat16)

    def feature_send(k):
        src_x, dst_x = 1 + 3 * core, 5 - 5 * core
        src_y, dst_y = 1 + 7 * half, 9 - 9 * half
        if k == 0:
            run = pl.ds(1 + 3 * half, 5)
            src, dst = xx.at[0, src_x, run], xx.at[0, dst_x, run]
            target = device_at(out_x, 0)
        elif k == 1:
            run = pl.ds(1 - core, 5)
            src, dst = xx.at[0, run, src_y], xx.at[0, run, dst_y]
            target = device_at(0, out_y)
        else:
            src, dst = xx.at[0, src_x, src_y], xx.at[0, dst_x, dst_y]
            target = device_at(out_x, out_y)
        return pltpu.make_async_remote_copy(
            src_ref=src,
            dst_ref=dst,
            send_sem=f_send.at[k],
            recv_sem=f_recv.at[k],
            device_id=target,
            device_id_type=MESH,
        )

    feature_when = (has_x, has_y, has_x & has_y)

    def turn(i, carry):
        xl = 4 * core + (1 - 2 * core) * i
        feature_load(xl).wait()
        value = stage[xl] * live_row
        xx[0, xl + 1 - core, 1:9] = jnp.transpose(value, (1, 0, 2))

        @pl.when(i == 0)
        def _():
            for k in (0, 2):

                @pl.when(feature_when[k])
                def _():
                    feature_send(k).start()

        return carry

    lax.fori_loop(0, 5, turn, 0)

    @pl.when(has_y)
    def _():
        feature_send(1).start()

    for k in range(3):
        weight_send(1, k).start()

    @pl.when(jnp.logical_not(has_x))
    def _():
        for layer in range(2):

            def clear(y, carry):
                xx[layer, 5 * core, y] = jnp.zeros((xx.shape[3], depth), xx.dtype)
                return carry

            lax.fori_loop(0, 10, clear, 0)

    @pl.when(jnp.logical_not(has_y))
    def _():
        for layer in range(2):

            def clear(x, carry):
                xx[layer, x, 9 * half] = jnp.zeros((xx.shape[3], depth), xx.dtype)
                return carry

            lax.fori_loop(0, 6, clear, 0)

    pltpu.make_async_copy(w_one, wall.at[0, chan], wl_sem.at[0]).wait()
    for k in range(3):
        bias_send(k).wait_recv()
        weight_send(0, k).wait_recv()
    rows = lax.broadcasted_iota(jnp.int32, (32, 128), 0)
    cols = lax.broadcasted_iota(jnp.int32, (32, 128), 1)
    for layer in range(2):
        for c in range(4):
            spread = jnp.broadcast_to(ball[c, layer : layer + 1, :], (32, 128))
            column_of = jnp.sum(
                jnp.where(rows == cols, spread, 0.0), axis=1, keepdims=True
            )
            bias[layer, 32 * c : 32 * c + 32] = jnp.broadcast_to(column_of, (32, 128))

    lane = lax.broadcasted_iota(jnp.int32, (128, depth), 1)

    def convolve(layer, px, py):
        rhs = jnp.concatenate(
            [xx[layer, px + i, base_y + py + j] for i in range(3) for j in range(3)],
            axis=0,
        )
        lhs = jnp.concatenate(
            [
                jnp.concatenate([wall[layer, c, 3 * t + k] for t in range(9)], axis=1)
                for k in range(3)
                for c in range(4)
            ],
            axis=0,
        )
        part = jnp.dot(lhs, rhs, preferred_element_type=jnp.float32)
        low = jnp.where(lane == 0, 0.0, pltpu.roll(part[0:128], 1, 1))
        high = jnp.where(lane == depth - 1, 0.0, pltpu.roll(part[256:384], depth - 1, 1))
        column_of = bias[layer]
        total = part[128:256] + low + high + jnp.concatenate([column_of] * (depth // 128), axis=1)
        total = jnp.where(lane < live_top, jnp.maximum(total, 0.0), 0.0)
        return total.astype(jnp.bfloat16)

    def first_place(n):
        late, last = n // 9, n // 13
        u = (1 - late) * (n // 3) + late * ((1 - last) * 3 + last * (n - 13))
        v = (1 - late) * (n % 3) + late * ((1 - last) * (n - 9) + last * 3)
        return (
            (1 - core) * 3 + (2 * core - 1) * u,
            (1 - half) * 3 + (2 * half - 1) * v,
        )

    def second_place(n):
        b, m = n // 4, n % 4
        e0, e3 = (3 - b) // 3, b // 3
        e2 = b // 2 - e3
        e1 = 1 - e0 - e2 - e3
        px = (e0 + e3) * (1 + m // 2) + 3 * e2
        py = e0 * (1 + m % 2) + (e1 + e2) * m + e3 * 3 * (m % 2)
        return px, py

    def hidden_send(d):
        dx, dy = DIRECTIONS[d]
        there = (fine_y + dy) % 2
        if dx == 0:
            src_x = dst_x = pl.ds(1, 4)
        else:
            src_x, dst_x = (4, 0) if dx > 0 else (1, 5)
        if dy == 0:
            src_y = dst_y = pl.ds(base_y + 1, 4)
        else:
            src_y = base_y + (4 if dy > 0 else 1)
            dst_y = 4 * there + (0 if dy > 0 else 5)
        return pltpu.make_async_remote_copy(
            src_ref=xx.at[1, src_x, src_y],
            dst_ref=xx.at[1, dst_x, dst_y],
            send_sem=h_send.at[d],
            recv_sem=h_recv.at[d],
            device_id=device_at(dx, dy),
            device_id_type=MESH,
        )

    def output_send(k, row=None):
        target = siblings[k]
        if row is None:
            src = obuf.at[target[1]]
            dst = out.at[pl.ds(4 * core, 4), pl.ds(4 * half, 4)]
        else:
            src = obuf.at[target[1], row]
            dst = out.at[4 * core + row, pl.ds(4 * half, 4)]
        return pltpu.make_async_remote_copy(
            src_ref=src,
            dst_ref=dst,
            send_sem=o_send.at[k],
            recv_sem=o_recv.at[k],
            device_id=target,
            device_id_type=MESH,
        )

    def first_pair(t, carry):
        @pl.when(t == 4)
        def _():
            for k in range(3):

                @pl.when(feature_when[k])
                def _():
                    feature_send(k).wait_recv()

        for q in range(2):
            px, py = first_place(2 * t + q)
            xx[1, px + 1, base_y + py + 1] = convolve(0, px, py)
        return carry

    lax.fori_loop(0, 8, first_pair, 0)

    for d, (dx, dy) in enumerate(DIRECTIONS):

        @pl.when(inside(dx, dy))
        def _():
            hidden_send(d).start()

    pltpu.make_async_copy(w_two, wall.at[1, chan], wl_sem.at[1]).wait()
    for k in range(3):
        weight_send(1, k).wait_recv()

    def second_pair(t, carry):
        @pl.when(t == 2)
        def _():
            for d, (dx, dy) in enumerate(DIRECTIONS):

                @pl.when(inside(-dx, -dy))
                def _():
                    hidden_send(d).wait_recv()

        for q in range(2):
            px, py = second_place(2 * t + q)
            value = convolve(1, px, py)
            for c in range(4):
                obuf[c, px, py] = value[32 * c : 32 * c + 32]

        for step, row in ((3, 0), (5, 3), (6, 1), (7, 2)):

            @pl.when(t == step)
            def _():
                for k in range(3):
                    output_send(k, row).start()

        return carry

    lax.fori_loop(0, 8, second_pair, 0)

    own = pltpu.make_async_copy(
        obuf.at[chan], out.at[pl.ds(4 * core, 4), pl.ds(4 * half, 4)], o_local
    )
    own.start()
    own.wait()
    for k in range(3):
        output_send(k).wait_recv()
    for k in range(3):
        output_send(k).wait_send()
        bias_send(k).wait_send()
        for layer in range(2):
            weight_send(layer, k).wait_send()

        @pl.when(feature_when[k])
        def _():
            feature_send(k).wait_send()

    for d, (dx, dy) in enumerate(DIRECTIONS):

        @pl.when(inside(dx, dy))
        def _():
            hidden_send(d).wait_send()


def on_device(features, column_heights, weight_one, bias_one, weight_two, bias_two):
    columns = lax.axis_size("space")
    depth = features.shape[4]
    bf16, f32 = jnp.bfloat16, jnp.float32
    anywhere = pl.BlockSpec(memory_space=pl.ANY)
    vmem = pl.BlockSpec(memory_space=pltpu.VMEM)
    smem = pl.BlockSpec(memory_space=pltpu.SMEM)
    dma = pltpu.SemaphoreType.DMA
    gathered = pl.pallas_call(
        functools.partial(kernel, columns // COL_Y, COL_Y),
        out_shape=jax.ShapeDtypeStruct((8, 8, 32, depth), bf16),
        in_specs=[anywhere, smem, anywhere, anywhere, vmem, vmem],
        out_specs=anywhere,
        scratch_shapes=[
            pltpu.VMEM((2, 6, 10, 128, depth), bf16),
            pltpu.VMEM((5, 128, 8, depth), bf16),
            pltpu.VMEM((2, 4, 27, 32, 128), bf16),
            pltpu.VMEM((8, 128), f32),
            pltpu.VMEM((4, 8, 128), f32),
            pltpu.VMEM((2, 128, 128), f32),
            pltpu.VMEM((4, 4, 4, 32, depth), bf16),
            dma((5,)),
            dma((2,)),
            dma((2, 3)),
            dma((2, 3)),
            dma((3,)),
            dma((3,)),
            dma((3,)),
            dma((3,)),
            dma((8,)),
            dma((8,)),
            dma((3,)),
            dma((3,)),
            dma,
        ],
        compiler_params=pltpu.CompilerParams(
            collective_id=0, has_side_effects=True, vmem_limit_bytes=60 << 20
        ),
        name="two_convolutions",
    )(
        features,
        column_heights,
        weight_one,
        weight_two,
        bias_one.reshape(1, 32),
        bias_two.reshape(1, 32),
    )
    return gathered.transpose(2, 0, 1, 3)[None]


def solution(mesh):
    placed = (
        P("space", None, None, None, None),
        P(),
        P(None, "chan", None),
        P("chan"),
        P(None, "chan", None),
        P("chan"),
    )
    return jax.shard_map(
        on_device,
        mesh=mesh,
        in_specs=placed,
        out_specs=P("space", "chan", None, None, None),
        check_vma=False,
    )
```

```python
import functools

import jax
import jax.numpy as jnp
from jax import lax
from jax.experimental import pallas as pl
from jax.experimental.pallas import tpu as pltpu
from jax.sharding import PartitionSpec as P

COL_Y = 8
MESH = pl.DeviceIdType.MESH
DIRECTIONS = [(dx, dy) for dx in (-1, 0, 1) for dy in (-1, 0, 1) if (dx, dy) != (0, 0)]
FIRST_ORDER = [
    (0, 0), (1, 0), (2, 0), (0, 1), (0, 2), (3, 0), (3, 1), (3, 2),
    (3, 3), (2, 3), (1, 3), (0, 3), (1, 1), (2, 1), (1, 2), (2, 2),
]
SECOND_ORDER = [
    (1, 1), (2, 1), (1, 2), (2, 2), (0, 1), (0, 2), (1, 0), (2, 0),
    (0, 0), (1, 3), (2, 3), (0, 3), (3, 1), (3, 2), (3, 0), (3, 3),
]
SECOND_WAITS = [
    (2, [(-1, 0)]),
    (3, [(0, -1)]),
    (4, [(-1, -1), (0, 1)]),
    (5, [(-1, 1)]),
    (6, [(1, 0)]),
    (7, [(1, -1), (1, 1)]),
]


def kernel(
    grid_x,
    grid_y,
    feat,
    heights,
    w_one,
    w_two,
    b_one,
    b_two,
    out,
    xx,
    stage,
    wall,
    bme,
    ball,
    bias,
    obuf,
    feat_sem,
    wl_sem,
    w_send,
    w_recv,
    b_send,
    b_recv,
    f_send,
    f_recv,
    h_send,
    h_recv,
    o_send,
    o_recv,
    o_local,
):
    column = lax.axis_index("space")
    chan = lax.axis_index("chan")
    core = chan % 2
    half = chan // 2
    col_x = column // grid_y
    col_y = column % grid_y
    fine_x = 2 * col_x + core
    fine_y = 2 * col_y + half
    depth = xx.shape[-1]
    base_y = 4 * half
    out_x = 2 * core - 1
    out_y = 2 * half - 1
    has_x = (col_x + out_x >= 0) & (col_x + out_x < grid_x)
    has_y = (col_y + out_y >= 0) & (col_y + out_y < grid_y)

    def device_at(a, b):
        fx, fy = fine_x + a * out_x, fine_y + b * out_y
        return ((fx // 2) * grid_y + fy // 2, (fy % 2) * 2 + fx % 2)

    def if_there(a, b):
        def run(action):
            if a == 1 and b == 1:
                pl.when(has_x & has_y)(action)
            elif a == 1:
                pl.when(has_x)(action)
            elif b == 1:
                pl.when(has_y)(action)
            else:
                action()

        return run

    def remote(src, dst, send_sem, recv_sem, target):
        return pltpu.make_async_remote_copy(
            src_ref=src,
            dst_ref=dst,
            send_sem=send_sem,
            recv_sem=recv_sem,
            device_id=target,
            device_id_type=MESH,
        )

    siblings = [
        (column, (1 - half) * 2 + core),
        (column, half * 2 + 1 - core),
        (column, (1 - half) * 2 + 1 - core),
    ]

    def feature_load(xl):
        return pltpu.make_async_copy(
            feat.at[0, :, 3 * core + xl], stage.at[xl], feat_sem.at[xl]
        )

    def turned(i):
        return 4 * core + (1 - 2 * core) * i

    for i in range(5):
        feature_load(turned(i)).start()
    weights = (w_one, w_two)

    def weight_load(layer):
        return pltpu.make_async_copy(
            weights[layer], wall.at[layer, chan], wl_sem.at[layer]
        )

    for layer in range(2):
        weight_load(layer).start()

    barrier = pltpu.get_barrier_semaphore()
    for a, b in DIRECTIONS:

        @if_there(a, b)
        def _():
            pl.semaphore_signal(
                barrier, inc=1, device_id=device_at(a, b), device_id_type=MESH
            )

    bme[...] = jnp.zeros_like(bme)
    bme[0:1, 0:32] = b_one[...]
    bme[1:2, 0:32] = b_two[...]
    ball[chan] = bme[...]

    live_top = heights[column] * 8
    lanes = lax.broadcasted_iota(jnp.int32, (1, 1, depth), 2)
    live_row = jnp.where(lanes < live_top, 1.0, 0.0).astype(jnp.bfloat16)

    def turn(i):
        xl = turned(i)
        feature_load(xl).wait()
        value = stage[xl] * live_row
        xx[0, xl + 1 - core, 1:9] = jnp.transpose(value, (1, 0, 2))

    def feature_send(a, b, i=None):
        src_x, dst_x = 1 + 3 * core, 5 - 5 * core
        src_y, dst_y = 1 + 7 * half, 9 - 9 * half
        if b == 0:
            run = pl.ds(1 + 3 * half, 5)
            src, dst = xx.at[0, src_x, run], xx.at[0, dst_x, run]
        elif a == 0:
            run = pl.ds(1 - core, 5) if i is None else turned(i) + 1 - core
            src, dst = xx.at[0, run, src_y], xx.at[0, run, dst_y]
        else:
            src, dst = xx.at[0, src_x, src_y], xx.at[0, dst_x, dst_y]
        k = a + 2 * b - 1
        return remote(src, dst, f_send.at[k], f_recv.at[k], device_at(a, b))

    FACES = ((1, 0), (0, 1), (1, 1))

    lax.fori_loop(0, 2, lambda i, carry: (turn(i), carry)[1], 0)

    def there(flag):
        return flag.astype(jnp.int32)

    pl.semaphore_wait(barrier, 3 + 2 * there(has_x) + 2 * there(has_y) + there(has_x & has_y))

    def weight_send(layer, k):
        share = chan if k < 2 else siblings[0][1]
        src = weights[layer] if k < 2 else wall.at[layer, share]
        return remote(
            src,
            wall.at[layer, share],
            w_send.at[layer, k],
            w_recv.at[layer, k],
            siblings[0 if k == 0 else 1],
        )

    def bias_send(k):
        return remote(bme, ball.at[chan], b_send.at[k], b_recv.at[k], siblings[k])

    for k in range(2):
        weight_send(0, k).start()
    for a, b in ((1, 0), (1, 1)):

        @if_there(a, b)
        def _():
            feature_send(a, b).start()

    for i in range(2):

        @if_there(0, 1)
        def _():
            feature_send(0, 1, i).start()

    for k in range(3):
        bias_send(k).start()

    def later_turn(i, carry):
        turn(i)

        @if_there(0, 1)
        def _():
            feature_send(0, 1, i).start()

        return carry

    lax.fori_loop(2, 5, later_turn, 0)

    @pl.when(jnp.logical_not(has_x))
    def _():
        for layer in range(2):

            def clear(y, carry):
                xx[layer, 5 * core, y] = jnp.zeros((xx.shape[3], depth), xx.dtype)
                return carry

            lax.fori_loop(0, 10, clear, 0)

    @pl.when(jnp.logical_not(has_y))
    def _():
        for layer in range(2):

            def clear(x, carry):
                xx[layer, x, 9 * half] = jnp.zeros((xx.shape[3], depth), xx.dtype)
                return carry

            lax.fori_loop(0, 6, clear, 0)

    def relay(layer):
        weight_send(layer, 0).wait_recv()
        weight_send(layer, 2).start()

    relay(0)
    for k in range(2):
        weight_send(1, k).start()

    for k in range(3):
        bias_send(k).wait_recv()
    rows = lax.broadcasted_iota(jnp.int32, (32, 128), 0)
    cols = lax.broadcasted_iota(jnp.int32, (32, 128), 1)
    for layer in range(2):
        for c in range(4):
            spread = jnp.broadcast_to(ball[c, layer : layer + 1, :], (32, 128))
            column_of = jnp.sum(
                jnp.where(rows == cols, spread, 0.0), axis=1, keepdims=True
            )
            bias[layer, 32 * c : 32 * c + 32] = jnp.broadcast_to(column_of, (32, 128))

    def weights_ready(layer):
        weight_load(layer).wait()
        weight_send(layer, 1).wait_recv()
        weight_send(layer, 2).wait_recv()

    weights_ready(0)

    lane = lax.broadcasted_iota(jnp.int32, (128, depth), 1)

    def convolve(layer, px, py):
        rhs = jnp.concatenate(
            [xx[layer, px + i, base_y + py + j] for i in range(3) for j in range(3)],
            axis=0,
        )
        lhs = jnp.concatenate(
            [
                jnp.concatenate([wall[layer, c, 3 * t + k] for t in range(9)], axis=1)
                for k in range(3)
                for c in range(4)
            ],
            axis=0,
        )
        part = jnp.dot(lhs, rhs, preferred_element_type=jnp.float32)
        low = jnp.where(lane == 0, 0.0, pltpu.roll(part[0:128], 1, 1))
        high = jnp.where(lane == depth - 1, 0.0, pltpu.roll(part[256:384], depth - 1, 1))
        column_of = bias[layer]
        total = part[128:256] + low + high + jnp.concatenate([column_of] * (depth // 128), axis=1)
        total = jnp.where(lane < live_top, jnp.maximum(total, 0.0), 0.0)
        return total.astype(jnp.bfloat16)

    def listed(n, table):
        found = table[0]
        for k in range(1, 16):
            if table[k] != table[k - 1]:
                found = found + (table[k] - table[k - 1]) * lax.div(n + (16 - k), 16)
        return found

    def place(order, n):
        u = listed(n, [p[0] for p in order])
        v = listed(n, [p[1] for p in order])
        px = (1 - core) * 3 + out_x * u
        py = (1 - half) * 3 + out_y * v
        return u, v, px, py

    def at_edge(a, b, u, v):
        flag = None
        for side, value in ((a, u), (b, v)):
            if side != 0:
                mine = value == (3 if side == 1 else 0)
                flag = mine if flag is None else flag & mine
        return flag

    def hidden_send(a, b, px, py):
        src_x, src_y = px + 1, py + 1
        dst_x = src_x - 4 * a * out_x
        dst_y = src_y - 4 * b * out_y
        there_y = half if b == 0 else 1 - half
        k = 3 * (a + 1) + b + 1
        return remote(
            xx.at[1, src_x, base_y + src_y],
            xx.at[1, dst_x, 4 * there_y + dst_y],
            h_send.at[k],
            h_recv.at[k],
            device_at(a, b),
        )

    def hidden_whole(a, b, arrived):
        def side(s, outer):
            if s == 0:
                return pl.ds(1, 4)
            edge = 5 * outer if s == 1 else 5 - 5 * outer
            return edge if arrived else 1 + 3 * (outer if s == 1 else 1 - outer)

        x, y = side(a, core), side(b, half)
        y = pl.ds(base_y + 1, 4) if b == 0 else base_y + y
        k = 3 * (a + 1) + b + 1
        return remote(xx.at[1, x, y], xx.at[1, x, y], h_send.at[k], h_recv.at[k], device_at(a, b))

    def output_send(k, px=None, py=None):
        target = siblings[k]
        if px is None:
            src = obuf.at[target[1]]
            dst = out.at[pl.ds(4 * core, 4), pl.ds(4 * half, 4)]
        else:
            src = obuf.at[target[1], px, py]
            dst = out.at[4 * core + px, 4 * half + py]
        return remote(src, dst, o_send.at[k], o_recv.at[k], target)

    def first_pair(t, carry):
        @pl.when(t == 2)
        def _():
            for a, b in FACES:

                @if_there(a, b)
                def _():
                    feature_send(a, b).wait_recv()

        @pl.when(t == 6)
        def _():
            relay(1)

        places = [place(FIRST_ORDER, 2 * t + q) for q in range(2)]
        for u, v, px, py in places:
            xx[1, px + 1, base_y + py + 1] = convolve(0, px, py)
        for u, v, px, py in places:
            for a, b in DIRECTIONS:

                @pl.when(at_edge(a, b, u, v))
                def _():
                    @if_there(a, b)
                    def _():
                        hidden_send(a, b, px, py).start()

        return carry

    lax.fori_loop(0, 8, first_pair, 0)

    weights_ready(1)

    def second_pair(t, carry):
        for step, sides in SECOND_WAITS:

            @pl.when(t == step)
            def _():
                for a, b in sides:

                    @if_there(a, b)
                    def _():
                        hidden_whole(a, b, True).wait_recv()

        places = [place(SECOND_ORDER, 2 * t + q) for q in range(2)]
        for u, v, px, py in places:
            value = convolve(1, px, py)
            for c in range(4):
                obuf[c, px, py] = value[32 * c : 32 * c + 32]
        for u, v, px, py in places:
            for k in (0, 2, 1):
                output_send(k, px, py).start()

        return carry

    lax.fori_loop(0, 8, second_pair, 0)

    own = pltpu.make_async_copy(
        obuf.at[chan], out.at[pl.ds(4 * core, 4), pl.ds(4 * half, 4)], o_local
    )
    own.start()
    for k in range(3):
        bias_send(k).wait_send()
        for layer in range(2):
            weight_send(layer, k).wait_send()
    for a, b in FACES:

        @if_there(a, b)
        def _():
            feature_send(a, b).wait_send()

    for a, b in DIRECTIONS:

        @if_there(a, b)
        def _():
            hidden_whole(a, b, False).wait_send()

    for k in range(3):
        output_send(k).wait_send()

    def arriving(k):
        target = siblings[k]
        there = (pl.ds(4 * (target[1] % 2), 4), pl.ds(4 * (target[1] // 2), 4))
        return remote(obuf.at[chan], out.at[there[0], there[1]], o_send.at[k], o_recv.at[k], target)

    for k in (1, 0, 2):
        arriving(k).wait_recv()
    own.wait()


def on_device(features, column_heights, weight_one, bias_one, weight_two, bias_two):
    columns = lax.axis_size("space")
    depth = features.shape[4]
    bf16, f32 = jnp.bfloat16, jnp.float32
    anywhere = pl.BlockSpec(memory_space=pl.ANY)
    vmem = pl.BlockSpec(memory_space=pltpu.VMEM)
    smem = pl.BlockSpec(memory_space=pltpu.SMEM)
    dma = pltpu.SemaphoreType.DMA
    gathered = pl.pallas_call(
        functools.partial(kernel, columns // COL_Y, COL_Y),
        out_shape=jax.ShapeDtypeStruct((8, 8, 32, depth), bf16),
        in_specs=[anywhere, smem, anywhere, anywhere, vmem, vmem],
        out_specs=anywhere,
        scratch_shapes=[
            pltpu.VMEM((2, 6, 10, 128, depth), bf16),
            pltpu.VMEM((5, 128, 8, depth), bf16),
            pltpu.VMEM((2, 4, 27, 32, 128), bf16),
            pltpu.VMEM((8, 128), f32),
            pltpu.VMEM((4, 8, 128), f32),
            pltpu.VMEM((2, 128, 128), f32),
            pltpu.VMEM((4, 4, 4, 32, depth), bf16),
            dma((5,)),
            dma((2,)),
            dma((2, 3)),
            dma((2, 3)),
            dma((3,)),
            dma((3,)),
            dma((3,)),
            dma((3,)),
            dma((9,)),
            dma((9,)),
            dma((3,)),
            dma((3,)),
            dma,
        ],
        compiler_params=pltpu.CompilerParams(
            collective_id=0, has_side_effects=True, vmem_limit_bytes=60 << 20
        ),
        name="two_convolutions",
    )(
        features,
        column_heights,
        weight_one,
        weight_two,
        bias_one.reshape(1, 32),
        bias_two.reshape(1, 32),
    )
    return gathered.transpose(2, 0, 1, 3)[None]


def solution(mesh):
    placed = (
        P("space", None, None, None, None),
        P(),
        P(None, "chan", None),
        P("chan"),
        P(None, "chan", None),
        P("chan"),
    )
    return jax.shard_map(
        on_device,
        mesh=mesh,
        in_specs=placed,
        out_specs=P("space", "chan", None, None, None),
        check_vma=False,
    )
```

```python
import functools

import jax
import jax.numpy as jnp
from jax import lax
from jax.experimental import pallas as pl
from jax.experimental.pallas import tpu as pltpu
from jax.sharding import PartitionSpec as P

COL_Y = 8
MESH = pl.DeviceIdType.MESH
DIRECTIONS = [(dx, dy) for dx in (-1, 0, 1) for dy in (-1, 0, 1) if (dx, dy) != (0, 0)]
FIRST_ORDER = [
    [(0, -1), (0, 0), (0, 1), (0, 2)],
    [(3, 3), (3, 2), (2, 3), (3, 1)],
    [(1, 3), (3, 0), (0, 3), (3, -1)],
    [(1, -1), (1, 0), (2, -1), (2, 0)],
    [(1, 1), (2, 1), (1, 2), (2, 2)],
]
SECOND_ORDER = [
    [(1, 0), (2, 0), (1, 1), (2, 1)],
    [(1, 2), (2, 2), (0, 0), (0, 1)],
    [(0, 2), (1, 3), (2, 3), (0, 3)],
    [(3, 0), (3, 1), (3, 2), (3, 3)],
]
SECOND_WAITS = [(1, [(-1, 0)]), (2, [(0, 1), (-1, 1)]), (3, [(1, 0), (1, 1)])]
HIDDEN = [(-1, 0), (1, 0), (0, 1), (-1, 1), (1, 1)]


def kernel(
    grid_x,
    grid_y,
    feat,
    heights,
    w_one,
    w_two,
    b_one,
    b_two,
    out,
    xx,
    stage,
    wall,
    bme,
    ball,
    bias,
    obuf,
    feat_sem,
    wl_sem,
    w_send,
    w_recv,
    b_send,
    b_recv,
    f_send,
    f_recv,
    h_send,
    h_recv,
    o_send,
    o_recv,
    o_local,
):
    column = lax.axis_index("space")
    chan = lax.axis_index("chan")
    core = chan % 2
    half = chan // 2
    col_x = column // grid_y
    col_y = column % grid_y
    fine_x = 2 * col_x + core
    fine_y = 2 * col_y + half
    depth = xx.shape[-1]
    base_y = 4 * half
    out_x = 2 * core - 1
    out_y = 2 * half - 1
    has_x = (col_x + out_x >= 0) & (col_x + out_x < grid_x)
    has_y = (col_y + out_y >= 0) & (col_y + out_y < grid_y)

    def device_at(a, b):
        fx, fy = fine_x + a * out_x, fine_y + b * out_y
        return ((fx // 2) * grid_y + fy // 2, (fy % 2) * 2 + fx % 2)

    def if_there(a, b):
        def run(action):
            if a == 1 and b == 1:
                pl.when(has_x & has_y)(action)
            elif a == 1:
                pl.when(has_x)(action)
            elif b == 1:
                pl.when(has_y)(action)
            else:
                action()

        return run

    def remote(src, dst, send_sem, recv_sem, target):
        return pltpu.make_async_remote_copy(
            src_ref=src,
            dst_ref=dst,
            send_sem=send_sem,
            recv_sem=recv_sem,
            device_id=target,
            device_id_type=MESH,
        )

    siblings = [
        (column, (1 - half) * 2 + core),
        (column, half * 2 + 1 - core),
        (column, (1 - half) * 2 + 1 - core),
    ]

    def feature_load(xl):
        return pltpu.make_async_copy(
            feat.at[0, :, 3 * core + xl], stage.at[xl], feat_sem.at[xl]
        )

    def turned(i):
        return 4 * core + (1 - 2 * core) * i

    for i in range(5):
        feature_load(turned(i)).start()
    weights = (w_one, w_two)

    def weight_load(layer):
        return pltpu.make_async_copy(
            weights[layer], wall.at[layer, chan], wl_sem.at[layer]
        )

    for layer in range(2):
        weight_load(layer).start()

    barrier = pltpu.get_barrier_semaphore()
    for a, b in DIRECTIONS:

        @if_there(a, b)
        def _():
            pl.semaphore_signal(
                barrier, inc=1, device_id=device_at(a, b), device_id_type=MESH
            )

    bme[...] = jnp.zeros_like(bme)
    bme[0:1, 0:32] = b_one[...]
    bme[1:2, 0:32] = b_two[...]
    ball[chan] = bme[...]

    live_top = heights[column] * 8
    lanes = lax.broadcasted_iota(jnp.int32, (1, 1, depth), 2)
    live_row = jnp.where(lanes < live_top, 1.0, 0.0).astype(jnp.bfloat16)

    def turn(i):
        xl = turned(i)
        feature_load(xl).wait()
        value = stage[xl] * live_row
        xx[0, xl + 1 - core, 1:9] = jnp.transpose(value, (1, 0, 2))

    def feature_send(a, b, i=None):
        src_x, dst_x = 1 + 3 * core, 5 - 5 * core
        src_y, dst_y = 1 + 7 * half, 9 - 9 * half
        if b == 0:
            run = pl.ds(1 + 2 * half, 6)
            src, dst = xx.at[0, src_x, run], xx.at[0, dst_x, run]
        elif a == 0:
            run = pl.ds(1 - core, 5) if i is None else turned(i) + 1 - core
            src, dst = xx.at[0, run, src_y], xx.at[0, run, dst_y]
        else:
            src, dst = xx.at[0, src_x, src_y], xx.at[0, dst_x, dst_y]
        k = a + 2 * b - 1
        return remote(src, dst, f_send.at[k], f_recv.at[k], device_at(a, b))

    FACES = ((1, 0), (0, 1), (1, 1))

    lax.fori_loop(0, 2, lambda i, carry: (turn(i), carry)[1], 0)

    def there(flag):
        return flag.astype(jnp.int32)

    pl.semaphore_wait(barrier, 3 + 2 * there(has_x) + 2 * there(has_y) + there(has_x & has_y))

    def weight_send(layer, k):
        share = chan if k < 2 else siblings[0][1]
        src = weights[layer] if k < 2 else wall.at[layer, share]
        return remote(
            src,
            wall.at[layer, share],
            w_send.at[layer, k],
            w_recv.at[layer, k],
            siblings[0 if k == 0 else 1],
        )

    def bias_send(k):
        return remote(bme, ball.at[chan], b_send.at[k], b_recv.at[k], siblings[k])

    for k in range(2):
        weight_send(0, k).start()
    for a, b in ((1, 0), (1, 1)):

        @if_there(a, b)
        def _():
            feature_send(a, b).start()

    for i in range(2):

        @if_there(0, 1)
        def _():
            feature_send(0, 1, i).start()

    for k in range(3):
        bias_send(k).start()

    def later_turn(i, carry):
        turn(i)

        @if_there(0, 1)
        def _():
            feature_send(0, 1, i).start()

        return carry

    lax.fori_loop(2, 5, later_turn, 0)

    @pl.when(jnp.logical_not(has_x))
    def _():
        for layer in range(2):

            def clear(y, carry):
                xx[layer, 5 * core, y] = jnp.zeros((xx.shape[3], depth), xx.dtype)
                return carry

            lax.fori_loop(0, 10, clear, 0)

    @pl.when(jnp.logical_not(has_y))
    def _():
        for layer in range(2):

            def clear(x, carry):
                xx[layer, x, 9 * half] = jnp.zeros((xx.shape[3], depth), xx.dtype)
                return carry

            lax.fori_loop(0, 6, clear, 0)

    def relay(layer):
        weight_send(layer, 0).wait_recv()
        weight_send(layer, 2).start()

    relay(0)
    for k in range(2):
        weight_send(1, k).start()

    for k in range(3):
        bias_send(k).wait_recv()
    rows = lax.broadcasted_iota(jnp.int32, (32, 128), 0)
    cols = lax.broadcasted_iota(jnp.int32, (32, 128), 1)
    for layer in range(2):
        for c in range(4):
            spread = jnp.broadcast_to(ball[c, layer : layer + 1, :], (32, 128))
            column_of = jnp.sum(
                jnp.where(rows == cols, spread, 0.0), axis=1, keepdims=True
            )
            bias[layer, 32 * c : 32 * c + 32] = jnp.broadcast_to(column_of, (32, 128))

    def weights_ready(layer):
        weight_load(layer).wait()
        weight_send(layer, 1).wait_recv()
        weight_send(layer, 2).wait_recv()

    weights_ready(0)

    lane = lax.broadcasted_iota(jnp.int32, (128, depth), 1)

    def convolve(layer, px, py):
        rhs = jnp.concatenate(
            [xx[layer, px + i, base_y + py + j] for i in range(3) for j in range(3)],
            axis=0,
        )
        lhs = jnp.concatenate(
            [
                jnp.concatenate([wall[layer, c, 3 * t + k] for t in range(9)], axis=1)
                for k in range(3)
                for c in range(4)
            ],
            axis=0,
        )
        part = jnp.dot(lhs, rhs, preferred_element_type=jnp.float32)
        low = jnp.where(lane == 0, 0.0, pltpu.roll(part[0:128], 1, 1))
        high = jnp.where(lane == depth - 1, 0.0, pltpu.roll(part[256:384], depth - 1, 1))
        column_of = bias[layer]
        total = part[128:256] + low + high + jnp.concatenate([column_of] * (depth // 128), axis=1)
        total = jnp.where(lane < live_top, jnp.maximum(total, 0.0), 0.0)
        return total.astype(jnp.bfloat16)

    def listed(t, table):
        found = table[0]
        for k in range(1, len(table)):
            if table[k] != table[k - 1]:
                found = found + (table[k] - table[k - 1]) * lax.div(t + (8 - k), 8)
        return found

    def places(order, t):
        found = []
        for q in range(4):
            u = listed(t, [group[q][0] for group in order])
            v = listed(t, [group[q][1] for group in order])
            px = (1 - core) * 3 + out_x * u
            py = (1 - half) * 3 + out_y * v
            found.append((u, v, px, py))
        return found

    def at_edge(a, b, u, v):
        flag = None
        for side, value in ((a, u), (b, v)):
            if side != 0:
                mine = value == (3 if side == 1 else 0)
                flag = mine if flag is None else flag & mine
        return flag

    def hidden_send(a, b, px, py):
        src_x, src_y = px + 1, py + 1
        dst_x = src_x - 4 * a * out_x
        dst_y = src_y - 4 * b * out_y
        there_y = half if b == 0 else 1 - half
        k = 3 * (a + 1) + b + 1
        return remote(
            xx.at[1, src_x, base_y + src_y],
            xx.at[1, dst_x, 4 * there_y + dst_y],
            h_send.at[k],
            h_recv.at[k],
            device_at(a, b),
        )

    def hidden_whole(a, b, arrived):
        def edge(s, outer):
            if arrived:
                return 5 * outer if s == 1 else 5 - 5 * outer
            return 1 + 3 * (outer if s == 1 else 1 - outer)

        x = pl.ds(1, 4) if a == 0 else edge(a, core)
        y = pl.ds(base_y + 1 - half, 5) if b == 0 else base_y + edge(b, half)
        k = 3 * (a + 1) + b + 1
        return remote(xx.at[1, x, y], xx.at[1, x, y], h_send.at[k], h_recv.at[k], device_at(a, b))

    def output_send(k, px=None, py=None):
        target = siblings[k]
        if px is None:
            src = obuf.at[target[1]]
            dst = out.at[pl.ds(4 * core, 4), pl.ds(4 * half, 4)]
        else:
            src = obuf.at[target[1], px, py]
            dst = out.at[4 * core + px, 4 * half + py]
        return remote(src, dst, o_send.at[k], o_recv.at[k], target)

    def first_step(t, carry):
        @pl.when(t == 1)
        def _():
            for a, b in FACES:

                @if_there(a, b)
                def _():
                    feature_send(a, b).wait_recv()

        @pl.when(t == 3)
        def _():
            relay(1)

        found = places(FIRST_ORDER, t)
        for u, v, px, py in found:
            xx[1, px + 1, base_y + py + 1] = convolve(0, px, py)
        for u, v, px, py in found:
            for a, b in HIDDEN:

                @pl.when(at_edge(a, b, u, v))
                def _():
                    @if_there(a, b)
                    def _():
                        hidden_send(a, b, px, py).start()

        return carry

    lax.fori_loop(0, len(FIRST_ORDER), first_step, 0)

    weights_ready(1)

    def second_step(t, carry):
        for step, sides in SECOND_WAITS:

            @pl.when(t == step)
            def _():
                for a, b in sides:

                    @if_there(a, b)
                    def _():
                        hidden_whole(a, b, True).wait_recv()

        found = places(SECOND_ORDER, t)
        for u, v, px, py in found:
            value = convolve(1, px, py)
            for c in range(4):
                obuf[c, px, py] = value[32 * c : 32 * c + 32]
        for u, v, px, py in found:
            for k in (0, 2, 1):
                output_send(k, px, py).start()

        return carry

    lax.fori_loop(0, len(SECOND_ORDER), second_step, 0)

    own = pltpu.make_async_copy(
        obuf.at[chan], out.at[pl.ds(4 * core, 4), pl.ds(4 * half, 4)], o_local
    )
    own.start()
    for k in range(3):
        bias_send(k).wait_send()
        for layer in range(2):
            weight_send(layer, k).wait_send()
    for a, b in FACES:

        @if_there(a, b)
        def _():
            feature_send(a, b).wait_send()

    for a, b in HIDDEN:

        @if_there(a, b)
        def _():
            hidden_whole(a, b, False).wait_send()

    for k in range(3):
        output_send(k).wait_send()

    def arriving(k):
        target = siblings[k]
        there = (pl.ds(4 * (target[1] % 2), 4), pl.ds(4 * (target[1] // 2), 4))
        return remote(obuf.at[chan], out.at[there[0], there[1]], o_send.at[k], o_recv.at[k], target)

    for k in (1, 0, 2):
        arriving(k).wait_recv()
    own.wait()


def on_device(features, column_heights, weight_one, bias_one, weight_two, bias_two):
    columns = lax.axis_size("space")
    depth = features.shape[4]
    bf16, f32 = jnp.bfloat16, jnp.float32
    anywhere = pl.BlockSpec(memory_space=pl.ANY)
    vmem = pl.BlockSpec(memory_space=pltpu.VMEM)
    smem = pl.BlockSpec(memory_space=pltpu.SMEM)
    dma = pltpu.SemaphoreType.DMA
    gathered = pl.pallas_call(
        functools.partial(kernel, columns // COL_Y, COL_Y),
        out_shape=jax.ShapeDtypeStruct((8, 8, 32, depth), bf16),
        in_specs=[anywhere, smem, anywhere, anywhere, vmem, vmem],
        out_specs=anywhere,
        scratch_shapes=[
            pltpu.VMEM((2, 6, 10, 128, depth), bf16),
            pltpu.VMEM((5, 128, 8, depth), bf16),
            pltpu.VMEM((2, 4, 27, 32, 128), bf16),
            pltpu.VMEM((8, 128), f32),
            pltpu.VMEM((4, 8, 128), f32),
            pltpu.VMEM((2, 128, 128), f32),
            pltpu.VMEM((4, 4, 4, 32, depth), bf16),
            dma((5,)),
            dma((2,)),
            dma((2, 3)),
            dma((2, 3)),
            dma((3,)),
            dma((3,)),
            dma((3,)),
            dma((3,)),
            dma((9,)),
            dma((9,)),
            dma((3,)),
            dma((3,)),
            dma,
        ],
        compiler_params=pltpu.CompilerParams(
            collective_id=0, has_side_effects=True, vmem_limit_bytes=60 << 20
        ),
        name="two_convolutions",
    )(
        features,
        column_heights,
        weight_one,
        weight_two,
        bias_one.reshape(1, 32),
        bias_two.reshape(1, 32),
    )
    return gathered.transpose(2, 0, 1, 3)[None]


def solution(mesh):
    placed = (
        P("space", None, None, None, None),
        P(),
        P(None, "chan", None),
        P("chan"),
        P(None, "chan", None),
        P("chan"),
    )
    return jax.shard_map(
        on_device,
        mesh=mesh,
        in_specs=placed,
        out_specs=P("space", "chan", None, None, None),
        check_vma=False,
    )
```

```python
import functools

import jax
import jax.numpy as jnp
from jax import lax
from jax.experimental import pallas as pl
from jax.experimental.pallas import tpu as pltpu
from jax.sharding import PartitionSpec as P

COL_Y = 8
MESH = pl.DeviceIdType.MESH
PARTNERS = [(-1, 0), (0, -1), (-1, -1), (1, 0), (0, 1), (1, 1)]
FIRST_ORDER = [
    [(0, -1), (0, 0), (0, 1), (0, 2)],
    [(1, -1), (1, 0), (2, -1), (2, 0)],
    [(3, 2), (2, 3), (3, 1), (1, 3)],
    [(3, 3), (3, 0), (0, 3), (3, -1)],
    [(1, 1), (2, 1), (1, 2), (2, 2)],
]
SECOND_ORDER = [
    [(1, 0), (2, 0), (1, 1), (2, 1)],
    [(1, 2), (2, 2), (0, 0), (0, 1)],
    [(3, 2), (2, 3), (3, 1), (1, 3)],
    [(0, 2), (0, 3), (3, 0), (3, 3)],
]
HIDDEN = [(-1, 0), (1, 0), (0, 1), (1, 1)]


def kernel(
    grid_x,
    grid_y,
    feat,
    heights,
    w_one,
    w_two,
    b_one,
    b_two,
    out,
    xx,
    stage,
    wall,
    bme,
    ball,
    bias,
    obuf,
    feat_sem,
    wl_sem,
    w_send,
    w_recv,
    b_send,
    b_recv,
    f_send,
    f_recv,
    h_send,
    h_recv,
    o_send,
    o_recv,
    o_local,
):
    column = lax.axis_index("space")
    chan = lax.axis_index("chan")
    core = chan % 2
    half = chan // 2
    col_x = column // grid_y
    col_y = column % grid_y
    fine_x = 2 * col_x + core
    fine_y = 2 * col_y + half
    depth = xx.shape[-1]
    base_y = 4 * half
    out_x = 2 * core - 1
    out_y = 2 * half - 1
    has_x = (col_x + out_x >= 0) & (col_x + out_x < grid_x)
    has_y = (col_y + out_y >= 0) & (col_y + out_y < grid_y)

    def device_at(a, b):
        fx, fy = fine_x + a * out_x, fine_y + b * out_y
        return ((fx // 2) * grid_y + fy // 2, (fy % 2) * 2 + fx % 2)

    def if_there(a, b):
        def run(action):
            if a == 1 and b == 1:
                pl.when(has_x & has_y)(action)
            elif a == 1:
                pl.when(has_x)(action)
            elif b == 1:
                pl.when(has_y)(action)
            else:
                action()

        return run

    def remote(src, dst, send_sem, recv_sem, target):
        return pltpu.make_async_remote_copy(
            src_ref=src,
            dst_ref=dst,
            send_sem=send_sem,
            recv_sem=recv_sem,
            device_id=target,
            device_id_type=MESH,
        )

    siblings = [
        (column, (1 - half) * 2 + core),
        (column, half * 2 + 1 - core),
        (column, (1 - half) * 2 + 1 - core),
    ]

    def feature_load(xl):
        return pltpu.make_async_copy(
            feat.at[0, :, 3 * core + xl], stage.at[xl], feat_sem.at[xl]
        )

    def turned(i):
        return 4 * core + (1 - 2 * core) * i

    for i in range(5):
        feature_load(turned(i)).start()
    weights = (w_one, w_two)

    def weight_load(layer):
        return pltpu.make_async_copy(
            weights[layer], wall.at[layer, chan], wl_sem.at[layer]
        )

    for layer in range(2):
        weight_load(layer).start()

    barrier = pltpu.get_barrier_semaphore()
    for a, b in PARTNERS:

        @if_there(a, b)
        def _():
            pl.semaphore_signal(
                barrier, inc=1, device_id=device_at(a, b), device_id_type=MESH
            )

    bme[...] = jnp.zeros_like(bme)
    bme[0:1, 0:32] = b_one[...]
    bme[1:2, 0:32] = b_two[...]
    ball[chan] = bme[...]

    live_top = heights[column] * 8
    lanes = lax.broadcasted_iota(jnp.int32, (1, 1, depth), 2)
    live_row = jnp.where(lanes < live_top, 1.0, 0.0).astype(jnp.bfloat16)

    def turn(i):
        xl = turned(i)
        feature_load(xl).wait()
        value = stage[xl] * live_row
        xx[0, xl + 1 - core, 1:9] = jnp.transpose(value, (1, 0, 2))

    def feature_send(a, b, i=None):
        src_x, dst_x = 1 + 3 * core, 5 - 5 * core
        src_y, dst_y = 1 + 7 * half, 9 - 9 * half
        if b == 0:
            run = pl.ds(1 + base_y, 4)
            src, dst = xx.at[0, src_x, run], xx.at[0, dst_x, run]
        elif a == 0:
            run = pl.ds(1, 4) if i is None else turned(i) + 1 - core
            src, dst = xx.at[0, run, src_y], xx.at[0, run, dst_y]
        else:
            src, dst = xx.at[0, src_x, src_y], xx.at[0, dst_x, dst_y]
        k = a + 2 * b - 1
        return remote(src, dst, f_send.at[k], f_recv.at[k], device_at(a, b))

    FACES = ((1, 0), (0, 1), (1, 1))

    def passed_on(layer, k, send_sem, recv_sem):
        if k == 0:
            rows = pl.ds(3 + 2 * half, 2) if layer == 0 else 4 + half
            src = dst = xx.at[layer, 5 * core, rows]
        else:
            src = xx.at[layer, 4 - 3 * core, 9 * half]
            dst = xx.at[layer, 5 * core, 9 * half]
        return remote(src, dst, send_sem, recv_sem, siblings[k])

    def feature_pass(k):
        return passed_on(0, k, f_send.at[3 + k], f_recv.at[3 + k])

    def hidden_pass(k):
        return passed_on(1, k, h_send.at[4 + k], h_recv.at[4 + k])

    lax.fori_loop(0, 2, lambda i, carry: (turn(i), carry)[1], 0)

    def there(flag):
        return flag.astype(jnp.int32)

    pl.semaphore_wait(barrier, 3 + there(has_x) + there(has_y) + there(has_x & has_y))

    def weight_send(layer, k):
        share = chan if k < 2 else siblings[0][1]
        src = weights[layer] if k < 2 else wall.at[layer, share]
        return remote(
            src,
            wall.at[layer, share],
            w_send.at[layer, k],
            w_recv.at[layer, k],
            siblings[0 if k == 0 else 1],
        )

    def bias_send(k):
        return remote(bme, ball.at[chan], b_send.at[k], b_recv.at[k], siblings[k])

    for k in range(2):
        weight_send(0, k).start()
    for a, b in ((1, 0), (1, 1)):

        @if_there(a, b)
        def _():
            feature_send(a, b).start()

    for i in range(2):

        @if_there(0, 1)
        def _():
            feature_send(0, 1, i).start()

    for k in range(3):
        bias_send(k).start()

    def later_turn(i, carry):
        turn(i)

        @if_there(0, 1)
        def _():
            feature_send(0, 1, i).start()

        return carry

    lax.fori_loop(2, 4, later_turn, 0)
    turn(4)

    @pl.when(jnp.logical_not(has_x))
    def _():
        for layer in range(2):

            def clear(y, carry):
                xx[layer, 5 * core, y] = jnp.zeros((xx.shape[3], depth), xx.dtype)
                return carry

            lax.fori_loop(0, 10, clear, 0)

    @pl.when(jnp.logical_not(has_y))
    def _():
        for layer in range(2):

            def clear(x, carry):
                xx[layer, x, 9 * half] = jnp.zeros((xx.shape[3], depth), xx.dtype)
                return carry

            lax.fori_loop(0, 6, clear, 0)

    def relay(layer):
        weight_send(layer, 0).wait_recv()
        weight_send(layer, 2).start()

    relay(0)
    for k in range(2):
        weight_send(1, k).start()

    for k in range(3):
        bias_send(k).wait_recv()
    rows = lax.broadcasted_iota(jnp.int32, (32, 128), 0)
    cols = lax.broadcasted_iota(jnp.int32, (32, 128), 1)
    for layer in range(2):
        for c in range(4):
            spread = jnp.broadcast_to(ball[c, layer : layer + 1, :], (32, 128))
            column_of = jnp.sum(
                jnp.where(rows == cols, spread, 0.0), axis=1, keepdims=True
            )
            bias[layer, 32 * c : 32 * c + 32] = jnp.broadcast_to(column_of, (32, 128))

    def weights_ready(layer):
        weight_load(layer).wait()
        weight_send(layer, 1).wait_recv()
        weight_send(layer, 2).wait_recv()

    weights_ready(0)

    lane = lax.broadcasted_iota(jnp.int32, (128, depth), 1)

    def convolve(layer, px, py):
        rhs = jnp.concatenate(
            [xx[layer, px + i, base_y + py + j] for i in range(3) for j in range(3)],
            axis=0,
        )
        lhs = jnp.concatenate(
            [
                jnp.concatenate([wall[layer, c, 3 * t + k] for t in range(9)], axis=1)
                for k in range(3)
                for c in range(4)
            ],
            axis=0,
        )
        part = jnp.dot(lhs, rhs, preferred_element_type=jnp.float32)
        low = jnp.where(lane == 0, 0.0, pltpu.roll(part[0:128], 1, 1))
        high = jnp.where(lane == depth - 1, 0.0, pltpu.roll(part[256:384], depth - 1, 1))
        column_of = bias[layer]
        total = part[128:256] + low + high + jnp.concatenate([column_of] * (depth // 128), axis=1)
        total = jnp.where(lane < live_top, jnp.maximum(total, 0.0), 0.0)
        return total.astype(jnp.bfloat16)

    def listed(t, table):
        found = table[0]
        for k in range(1, len(table)):
            if table[k] != table[k - 1]:
                found = found + (table[k] - table[k - 1]) * lax.div(t + (8 - k), 8)
        return found

    def places(order, t):
        found = []
        for q in range(4):
            u = listed(t, [group[q][0] for group in order])
            v = listed(t, [group[q][1] for group in order])
            px = (1 - core) * 3 + out_x * u
            py = (1 - half) * 3 + out_y * v
            found.append((u, v, px, py))
        return found

    def at_edge(a, b, u, v):
        flag = None
        for side, value in ((a, u), (b, v)):
            if side != 0:
                mine = value == (3 if side == 1 else 0)
                flag = mine if flag is None else flag & mine
        if (a, b) == (1, 0):
            flag = flag & (v >= 0)
        return flag

    def hidden_send(a, b, px, py):
        src_x, src_y = px + 1, py + 1
        dst_x = src_x - 4 * a * out_x
        dst_y = src_y - 4 * b * out_y
        there_y = half if b == 0 else 1 - half
        k = HIDDEN.index((a, b))
        return remote(
            xx.at[1, src_x, base_y + src_y],
            xx.at[1, dst_x, 4 * there_y + dst_y],
            h_send.at[k],
            h_recv.at[k],
            device_at(a, b),
        )

    def hidden_whole(a, b, arrived):
        def edge(s, outer):
            if arrived:
                return 5 * outer if s == 1 else 5 - 5 * outer
            return 1 + 3 * (outer if s == 1 else 1 - outer)

        x = pl.ds(1, 4) if a == 0 else edge(a, core)
        if b != 0:
            y = base_y + edge(b, half)
        else:
            y = pl.ds(base_y + 1, 4) if a == 1 else pl.ds(base_y + 1 - half, 5)
        k = HIDDEN.index((a, b))
        return remote(xx.at[1, x, y], xx.at[1, x, y], h_send.at[k], h_recv.at[k], device_at(a, b))

    def output_send(k, px=None, py=None):
        target = siblings[k]
        if px is None:
            src = obuf.at[target[1]]
            dst = out.at[pl.ds(4 * core, 4), pl.ds(4 * half, 4)]
        else:
            src = obuf.at[target[1], px, py]
            dst = out.at[4 * core + px, 4 * half + py]
        return remote(src, dst, o_send.at[k], o_recv.at[k], target)

    def first_step(t, carry):
        @pl.when(t == 2)
        def _():
            for k, (a, b) in enumerate(FACES[:2]):

                @if_there(a, b)
                def _():
                    feature_send(a, b).wait_recv()
                    feature_pass(k).start()

            relay(1)

        @pl.when(t == 3)
        def _():
            for k, (a, b) in enumerate(FACES[:2]):

                @if_there(a, b)
                def _():
                    feature_pass(k).wait_recv()

            @if_there(1, 1)
            def _():
                feature_send(1, 1).wait_recv()

        found = places(FIRST_ORDER, t)
        values = [convolve(0, px, py) for u, v, px, py in found]
        for (u, v, px, py), value in zip(found, values):
            xx[1, px + 1, base_y + py + 1] = value
        for u, v, px, py in found:
            for a, b in HIDDEN:

                @pl.when(at_edge(a, b, u, v))
                def _():
                    @if_there(a, b)
                    def _():
                        hidden_send(a, b, px, py).start()

        return carry

    lax.fori_loop(0, len(FIRST_ORDER), first_step, 0)

    weights_ready(1)

    def second_step(t, carry):
        @pl.when(t == 1)
        def _():
            hidden_whole(-1, 0, True).wait_recv()

        @pl.when(t == 2)
        def _():
            for k, (a, b) in enumerate(FACES[:2]):

                @if_there(a, b)
                def _():
                    hidden_whole(a, b, True).wait_recv()
                    hidden_pass(k).start()

        @pl.when(t == 3)
        def _():
            for k, (a, b) in enumerate(FACES[:2]):

                @if_there(a, b)
                def _():
                    hidden_pass(k).wait_recv()

            @if_there(1, 1)
            def _():
                hidden_whole(1, 1, True).wait_recv()

        found = places(SECOND_ORDER, t)
        values = [convolve(1, px, py) for u, v, px, py in found]
        for (u, v, px, py), value in zip(found, values):
            for c in range(4):
                obuf[c, px, py] = value[32 * c : 32 * c + 32]
        for u, v, px, py in found:
            for k in (0, 2, 1):
                output_send(k, px, py).start()

        return carry

    lax.fori_loop(0, len(SECOND_ORDER), second_step, 0)

    own = pltpu.make_async_copy(
        obuf.at[chan], out.at[pl.ds(4 * core, 4), pl.ds(4 * half, 4)], o_local
    )
    own.start()
    for k in range(3):
        bias_send(k).wait_send()
        for layer in range(2):
            weight_send(layer, k).wait_send()
    for a, b in FACES:

        @if_there(a, b)
        def _():
            feature_send(a, b).wait_send()

    for k, (a, b) in enumerate(FACES[:2]):

        @if_there(a, b)
        def _():
            feature_pass(k).wait_send()
            hidden_pass(k).wait_send()

    for a, b in HIDDEN:

        @if_there(a, b)
        def _():
            hidden_whole(a, b, False).wait_send()

    for k in range(3):
        output_send(k).wait_send()

    def arriving(k):
        target = siblings[k]
        there = (pl.ds(4 * (target[1] % 2), 4), pl.ds(4 * (target[1] // 2), 4))
        return remote(obuf.at[chan], out.at[there[0], there[1]], o_send.at[k], o_recv.at[k], target)

    for k in (1, 0, 2):
        arriving(k).wait_recv()
    own.wait()


def on_device(features, column_heights, weight_one, bias_one, weight_two, bias_two):
    columns = lax.axis_size("space")
    depth = features.shape[4]
    bf16, f32 = jnp.bfloat16, jnp.float32
    anywhere = pl.BlockSpec(memory_space=pl.ANY)
    vmem = pl.BlockSpec(memory_space=pltpu.VMEM)
    smem = pl.BlockSpec(memory_space=pltpu.SMEM)
    dma = pltpu.SemaphoreType.DMA
    gathered = pl.pallas_call(
        functools.partial(kernel, columns // COL_Y, COL_Y),
        out_shape=jax.ShapeDtypeStruct((8, 8, 32, depth), bf16),
        in_specs=[anywhere, smem, anywhere, anywhere, vmem, vmem],
        out_specs=anywhere,
        scratch_shapes=[
            pltpu.VMEM((2, 6, 10, 128, depth), bf16),
            pltpu.VMEM((5, 128, 8, depth), bf16),
            pltpu.VMEM((2, 4, 27, 32, 128), bf16),
            pltpu.VMEM((8, 128), f32),
            pltpu.VMEM((4, 8, 128), f32),
            pltpu.VMEM((2, 128, 128), f32),
            pltpu.VMEM((4, 4, 4, 32, depth), bf16),
            dma((5,)),
            dma((2,)),
            dma((2, 3)),
            dma((2, 3)),
            dma((3,)),
            dma((3,)),
            dma((5,)),
            dma((5,)),
            dma((6,)),
            dma((6,)),
            dma((3,)),
            dma((3,)),
            dma,
        ],
        compiler_params=pltpu.CompilerParams(
            collective_id=0, has_side_effects=True, vmem_limit_bytes=60 << 20
        ),
        name="two_convolutions",
    )(
        features,
        column_heights,
        weight_one,
        weight_two,
        bias_one.reshape(1, 32),
        bias_two.reshape(1, 32),
    )
    return gathered.transpose(2, 0, 1, 3)[None]


def solution(mesh):
    placed = (
        P("space", None, None, None, None),
        P(),
        P(None, "chan", None),
        P("chan"),
        P(None, "chan", None),
        P("chan"),
    )
    return jax.shard_map(
        on_device,
        mesh=mesh,
        in_specs=placed,
        out_specs=P("space", "chan", None, None, None),
        check_vma=False,
    )
```

```python
import functools

import jax
import jax.numpy as jnp
from jax import lax
from jax.experimental import pallas as pl
from jax.experimental.pallas import tpu as pltpu
from jax.sharding import PartitionSpec as P

COL_Y = 8
MESH = pl.DeviceIdType.MESH
PARTNERS = [(-1, 0), (0, -1), (-1, -1), (1, 0), (0, 1)]
FIRST_ORDER = [
    [(0, -1), (0, 0), (0, 1), (0, 2)],
    [(1, -1), (1, 0), (2, -1), (2, 0)],
    [(1, 1), (2, 1), (1, 2), (2, 2)],
    [(3, 2), (2, 3), (3, 1), (1, 3)],
    [(3, 3), (3, 0), (0, 3), (3, -1)],
]
SECOND_ORDER = [
    [(1, 0), (2, 0), (1, 1), (2, 1)],
    [(1, 2), (2, 2), (0, 0), (0, 1)],
    [(3, 2), (2, 3), (3, 1), (1, 3)],
    [(0, 2), (0, 3), (3, 0), (3, 3)],
]
HIDDEN = [(-1, 0), (1, 0), (0, 1)]


def kernel(
    grid_x,
    grid_y,
    feat,
    heights,
    w_one,
    w_two,
    b_one,
    b_two,
    out,
    xx,
    stage,
    wall,
    bme,
    ball,
    bias,
    obuf,
    feat_sem,
    wl_sem,
    w_send,
    w_recv,
    b_send,
    b_recv,
    f_send,
    f_recv,
    h_send,
    h_recv,
    o_send,
    o_recv,
    o_local,
):
    column = lax.axis_index("space")
    chan = lax.axis_index("chan")
    core = chan % 2
    half = chan // 2
    col_x = column // grid_y
    col_y = column % grid_y
    fine_x = 2 * col_x + core
    fine_y = 2 * col_y + half
    depth = xx.shape[-1]
    base_y = 4 * half
    out_x = 2 * core - 1
    out_y = 2 * half - 1
    has_x = (col_x + out_x >= 0) & (col_x + out_x < grid_x)
    has_y = (col_y + out_y >= 0) & (col_y + out_y < grid_y)

    def device_at(a, b):
        fx, fy = fine_x + a * out_x, fine_y + b * out_y
        return ((fx // 2) * grid_y + fy // 2, (fy % 2) * 2 + fx % 2)

    def if_there(a, b):
        def run(action):
            if a == 1 and b == 1:
                pl.when(has_x & has_y)(action)
            elif a == 1:
                pl.when(has_x)(action)
            elif b == 1:
                pl.when(has_y)(action)
            else:
                action()

        return run

    def remote(src, dst, send_sem, recv_sem, target):
        return pltpu.make_async_remote_copy(
            src_ref=src,
            dst_ref=dst,
            send_sem=send_sem,
            recv_sem=recv_sem,
            device_id=target,
            device_id_type=MESH,
        )

    siblings = [
        (column, (1 - half) * 2 + core),
        (column, half * 2 + 1 - core),
        (column, (1 - half) * 2 + 1 - core),
    ]

    def feature_load(xl):
        return pltpu.make_async_copy(
            feat.at[0, :, 3 * core + xl], stage.at[xl], feat_sem.at[xl]
        )

    def turned(i):
        return 4 * core + (1 - 2 * core) * i

    for i in range(5):
        feature_load(turned(i)).start()
    weights = (w_one, w_two)

    def weight_load(layer):
        return pltpu.make_async_copy(
            weights[layer], wall.at[layer, chan], wl_sem.at[layer]
        )

    for layer in range(2):
        weight_load(layer).start()

    barrier = pltpu.get_barrier_semaphore()
    for a, b in PARTNERS:

        @if_there(a, b)
        def _():
            pl.semaphore_signal(
                barrier, inc=1, device_id=device_at(a, b), device_id_type=MESH
            )

    bme[...] = jnp.zeros_like(bme)
    bme[0:1, 0:32] = b_one[...]
    bme[1:2, 0:32] = b_two[...]
    ball[chan] = bme[...]

    live_top = heights[column] * 8
    lanes = lax.broadcasted_iota(jnp.int32, (1, 1, depth), 2)
    live_row = jnp.where(lanes < live_top, 1.0, 0.0).astype(jnp.bfloat16)

    def turn(i):
        xl = turned(i)
        feature_load(xl).wait()
        value = stage[xl] * live_row
        xx[0, xl + 1 - core, 1:9] = jnp.transpose(value, (1, 0, 2))

    def feature_send(a, b, i=None):
        src_x, dst_x = 1 + 3 * core, 5 - 5 * core
        src_y, dst_y = 1 + 7 * half, 9 - 9 * half
        if b == 0:
            run = pl.ds(1 + base_y, 4)
            src, dst = xx.at[0, src_x, run], xx.at[0, dst_x, run]
        else:
            run = pl.ds(1, 4) if i is None else turned(i) + 1 - core
            src, dst = xx.at[0, run, src_y], xx.at[0, run, dst_y]
        k = b
        return remote(src, dst, f_send.at[k], f_recv.at[k], device_at(a, b))

    FACES = ((1, 0), (0, 1))

    def passed_on(layer, k, send_sem, recv_sem):
        if k == 0:
            rows = pl.ds(3 + 2 * half, 2) if layer == 0 else 4 + half
            src = dst = xx.at[layer, 5 * core, rows]
        elif k == 1:
            src = xx.at[layer, 4 - 3 * core, 9 * half]
            dst = xx.at[layer, 5 * core, 9 * half]
        else:
            src = xx.at[layer, 5 * core, 1 + 7 * half]
            dst = xx.at[layer, 5 * core, 9 - 9 * half]
        return remote(src, dst, send_sem, recv_sem, device_at(0, 1) if k == 2 else siblings[k])

    def feature_pass(k):
        return passed_on(0, k, f_send.at[2 + k], f_recv.at[2 + k])

    def hidden_pass(k):
        return passed_on(1, k, h_send.at[3 + k], h_recv.at[3 + k])

    lax.fori_loop(0, 2, lambda i, carry: (turn(i), carry)[1], 0)

    def there(flag):
        return flag.astype(jnp.int32)

    pl.semaphore_wait(barrier, 3 + there(has_x) + there(has_y))

    def weight_send(layer, k):
        share = chan if k < 2 else siblings[0][1]
        src = weights[layer] if k < 2 else wall.at[layer, share]
        return remote(
            src,
            wall.at[layer, share],
            w_send.at[layer, k],
            w_recv.at[layer, k],
            siblings[0 if k == 0 else 1],
        )

    def bias_send(k):
        return remote(bme, ball.at[chan], b_send.at[k], b_recv.at[k], siblings[k])

    for k in range(2):
        weight_send(0, k).start()

    @if_there(1, 0)
    def _():
        feature_send(1, 0).start()

    for i in range(2):

        @if_there(0, 1)
        def _():
            feature_send(0, 1, i).start()

    for k in range(3):
        bias_send(k).start()

    def later_turn(i, carry):
        turn(i)

        @if_there(0, 1)
        def _():
            feature_send(0, 1, i).start()

        return carry

    lax.fori_loop(2, 4, later_turn, 0)
    turn(4)

    @pl.when(jnp.logical_not(has_x))
    def _():
        for layer in range(2):

            def clear(y, carry):
                xx[layer, 5 * core, y] = jnp.zeros((xx.shape[3], depth), xx.dtype)
                return carry

            lax.fori_loop(0, 10, clear, 0)

    @pl.when(jnp.logical_not(has_y))
    def _():
        for layer in range(2):

            def clear(x, carry):
                xx[layer, x, 9 * half] = jnp.zeros((xx.shape[3], depth), xx.dtype)
                return carry

            lax.fori_loop(0, 6, clear, 0)

    def relay(layer):
        weight_send(layer, 0).wait_recv()
        weight_send(layer, 2).start()

    relay(0)
    for k in range(2):
        weight_send(1, k).start()

    for k in range(3):
        bias_send(k).wait_recv()
    rows = lax.broadcasted_iota(jnp.int32, (32, 128), 0)
    cols = lax.broadcasted_iota(jnp.int32, (32, 128), 1)
    for layer in range(2):
        for c in range(4):
            spread = jnp.broadcast_to(ball[c, layer : layer + 1, :], (32, 128))
            column_of = jnp.sum(
                jnp.where(rows == cols, spread, 0.0), axis=1, keepdims=True
            )
            bias[layer, 32 * c : 32 * c + 32] = jnp.broadcast_to(column_of, (32, 128))

    def weights_ready(layer):
        weight_load(layer).wait()
        weight_send(layer, 1).wait_recv()
        weight_send(layer, 2).wait_recv()

    weights_ready(0)

    lane = lax.broadcasted_iota(jnp.int32, (128, depth), 1)

    def convolve(layer, px, py):
        rhs = jnp.concatenate(
            [xx[layer, px + i, base_y + py + j] for i in range(3) for j in range(3)],
            axis=0,
        )
        lhs = jnp.concatenate(
            [
                jnp.concatenate([wall[layer, c, 3 * t + k] for t in range(9)], axis=1)
                for k in range(3)
                for c in range(4)
            ],
            axis=0,
        )
        part = jnp.dot(lhs, rhs, preferred_element_type=jnp.float32)
        low = jnp.where(lane == 0, 0.0, pltpu.roll(part[0:128], 1, 1))
        high = jnp.where(lane == depth - 1, 0.0, pltpu.roll(part[256:384], depth - 1, 1))
        column_of = bias[layer]
        total = part[128:256] + low + high + jnp.concatenate([column_of] * (depth // 128), axis=1)
        total = jnp.where(lane < live_top, jnp.maximum(total, 0.0), 0.0)
        return total.astype(jnp.bfloat16)

    def listed(t, table):
        found = table[0]
        for k in range(1, len(table)):
            if table[k] != table[k - 1]:
                found = found + (table[k] - table[k - 1]) * lax.div(t + (8 - k), 8)
        return found

    def places(order, t):
        found = []
        for q in range(4):
            u = listed(t, [group[q][0] for group in order])
            v = listed(t, [group[q][1] for group in order])
            px = (1 - core) * 3 + out_x * u
            py = (1 - half) * 3 + out_y * v
            found.append((u, v, px, py))
        return found

    def at_edge(a, b, u, v):
        flag = None
        for side, value in ((a, u), (b, v)):
            if side != 0:
                mine = value == (3 if side == 1 else 0)
                flag = mine if flag is None else flag & mine
        return flag

    def hidden_send(a, b, px, py):
        src_x, src_y = px + 1, py + 1
        dst_x = src_x - 4 * a * out_x
        dst_y = src_y - 4 * b * out_y
        there_y = half if b == 0 else 1 - half
        k = HIDDEN.index((a, b))
        return remote(
            xx.at[1, src_x, base_y + src_y],
            xx.at[1, dst_x, 4 * there_y + dst_y],
            h_send.at[k],
            h_recv.at[k],
            device_at(a, b),
        )

    def hidden_whole(a, b, arrived):
        def edge(s, outer):
            if arrived:
                return 5 * outer if s == 1 else 5 - 5 * outer
            return 1 + 3 * (outer if s == 1 else 1 - outer)

        x = pl.ds(1, 4) if a == 0 else edge(a, core)
        if b != 0:
            y = base_y + edge(b, half)
        else:
            y = pl.ds(base_y + 1 - half, 5)
        k = HIDDEN.index((a, b))
        return remote(xx.at[1, x, y], xx.at[1, x, y], h_send.at[k], h_recv.at[k], device_at(a, b))

    def output_send(k, px=None, py=None):
        target = siblings[k]
        if px is None:
            src = obuf.at[target[1]]
            dst = out.at[pl.ds(4 * core, 4), pl.ds(4 * half, 4)]
        else:
            src = obuf.at[target[1], px, py]
            dst = out.at[4 * core + px, 4 * half + py]
        return remote(src, dst, o_send.at[k], o_recv.at[k], target)

    def first_step(t, carry):
        @pl.when(t == 3)
        def _():
            for k, (a, b) in enumerate(FACES):

                @if_there(a, b)
                def _():
                    feature_send(a, b).wait_recv()
                    feature_pass(k).start()

                if k == 0:

                    @if_there(1, 1)
                    def _():
                        feature_pass(2).start()

            relay(1)

        @pl.when(t == 4)
        def _():
            for k, (a, b) in enumerate(FACES):

                @if_there(a, b)
                def _():
                    feature_pass(k).wait_recv()

            @if_there(1, 1)
            def _():
                feature_pass(2).wait_recv()

        found = places(FIRST_ORDER, t)
        values = [convolve(0, px, py) for u, v, px, py in found]
        for (u, v, px, py), value in zip(found, values):
            xx[1, px + 1, base_y + py + 1] = value
        for u, v, px, py in found:
            for a, b in HIDDEN:

                @pl.when(at_edge(a, b, u, v))
                def _():
                    @if_there(a, b)
                    def _():
                        hidden_send(a, b, px, py).start()

        return carry

    lax.fori_loop(0, len(FIRST_ORDER), first_step, 0)

    weights_ready(1)

    def second_step(t, carry):
        @pl.when(t == 1)
        def _():
            hidden_whole(-1, 0, True).wait_recv()

        @pl.when(t == 2)
        def _():
            for k, (a, b) in enumerate(FACES):

                @if_there(a, b)
                def _():
                    hidden_whole(a, b, True).wait_recv()
                    if k == 1:
                        hidden_pass(1).start()

                if k == 0:

                    @if_there(1, 1)
                    def _():
                        hidden_pass(2).start()

        @pl.when(t == 3)
        def _():
            @if_there(0, 1)
            def _():
                hidden_pass(1).wait_recv()

            @if_there(1, 1)
            def _():
                hidden_pass(2).wait_recv()

        found = places(SECOND_ORDER, t)
        values = [convolve(1, px, py) for u, v, px, py in found]
        for (u, v, px, py), value in zip(found, values):
            for c in range(4):
                obuf[c, px, py] = value[32 * c : 32 * c + 32]
        for u, v, px, py in found:
            for k in (0, 2, 1):
                output_send(k, px, py).start()

        return carry

    lax.fori_loop(0, len(SECOND_ORDER), second_step, 0)

    own = pltpu.make_async_copy(
        obuf.at[chan], out.at[pl.ds(4 * core, 4), pl.ds(4 * half, 4)], o_local
    )
    own.start()
    for k in range(3):
        bias_send(k).wait_send()
        for layer in range(2):
            weight_send(layer, k).wait_send()
    for a, b in FACES:

        @if_there(a, b)
        def _():
            feature_send(a, b).wait_send()

    for k, (a, b) in enumerate(FACES):

        @if_there(a, b)
        def _():
            feature_pass(k).wait_send()
            if k == 1:
                hidden_pass(1).wait_send()

    @if_there(1, 1)
    def _():
        feature_pass(2).wait_send()
        hidden_pass(2).wait_send()

    for a, b in HIDDEN:

        @if_there(a, b)
        def _():
            hidden_whole(a, b, False).wait_send()

    for k in range(3):
        output_send(k).wait_send()

    def arriving(k):
        target = siblings[k]
        there = (pl.ds(4 * (target[1] % 2), 4), pl.ds(4 * (target[1] // 2), 4))
        return remote(obuf.at[chan], out.at[there[0], there[1]], o_send.at[k], o_recv.at[k], target)

    for k in (1, 0, 2):
        arriving(k).wait_recv()
    own.wait()


def settle(gathered, out):
    rows = out.shape[2]
    for x in range(rows):
        out[0, :, x] = jnp.transpose(gathered[pl.program_id(0) * rows + x], (1, 0, 2))


def on_device(features, column_heights, weight_one, bias_one, weight_two, bias_two):
    columns = lax.axis_size("space")
    depth = features.shape[4]
    bf16, f32 = jnp.bfloat16, jnp.float32
    anywhere = pl.BlockSpec(memory_space=pl.ANY)
    vmem = pl.BlockSpec(memory_space=pltpu.VMEM)
    smem = pl.BlockSpec(memory_space=pltpu.SMEM)
    dma = pltpu.SemaphoreType.DMA
    gathered = pl.pallas_call(
        functools.partial(kernel, columns // COL_Y, COL_Y),
        out_shape=jax.ShapeDtypeStruct((8, 8, 32, depth), bf16),
        in_specs=[anywhere, smem, anywhere, anywhere, vmem, vmem],
        out_specs=anywhere,
        scratch_shapes=[
            pltpu.VMEM((2, 6, 10, 128, depth), bf16),
            pltpu.VMEM((5, 128, 8, depth), bf16),
            pltpu.VMEM((2, 4, 27, 32, 128), bf16),
            pltpu.VMEM((8, 128), f32),
            pltpu.VMEM((4, 8, 128), f32),
            pltpu.VMEM((2, 128, 128), f32),
            pltpu.VMEM((4, 4, 4, 32, depth), bf16),
            dma((5,)),
            dma((2,)),
            dma((2, 3)),
            dma((2, 3)),
            dma((3,)),
            dma((3,)),
            dma((5,)),
            dma((5,)),
            dma((6,)),
            dma((6,)),
            dma((3,)),
            dma((3,)),
            dma,
        ],
        compiler_params=pltpu.CompilerParams(
            collective_id=0, has_side_effects=True, vmem_limit_bytes=60 << 20
        ),
        name="two_convolutions",
    )(
        features,
        column_heights,
        weight_one,
        weight_two,
        bias_one.reshape(1, 32),
        bias_two.reshape(1, 32),
    )
    return pl.pallas_call(
        settle,
        grid=(2,),
        out_shape=jax.ShapeDtypeStruct((1, 32, 8, 8, depth), bf16),
        in_specs=[vmem],
        out_specs=pl.BlockSpec((1, 32, 4, 8, depth), lambda x: (0, 0, x, 0, 0)),
        name="settle",
    )(gathered)


def solution(mesh):
    placed = (
        P("space", None, None, None, None),
        P(),
        P(None, "chan", None),
        P("chan"),
        P(None, "chan", None),
        P("chan"),
    )
    return jax.shard_map(
        on_device,
        mesh=mesh,
        in_specs=placed,
        out_specs=P("space", "chan", None, None, None),
        check_vma=False,
    )
```

```python
import functools

import jax
import jax.numpy as jnp
from jax import lax
from jax.experimental import pallas as pl
from jax.experimental.pallas import tpu as pltpu
from jax.sharding import PartitionSpec as P

COL_Y = 8
MESH = pl.DeviceIdType.MESH
PARTNERS = [(-1, 0), (0, -1), (-1, -1), (1, 0), (0, 1)]
FIRST_ORDER = [
    [(0, -1), (0, 0), (0, 1), (0, 2)],
    [(1, -1), (1, 0), (2, -1), (2, 0)],
    [(1, 1), (2, 1), (1, 2), (2, 2)],
    [(3, 1), (3, 2), (2, 3), (1, 3)],
    [(3, -1), (3, 0), (3, 3), (0, 3)],
]
SECOND_ORDER = [
    [(1, 0), (2, 0), (1, 1), (2, 1)],
    [(1, 2), (2, 2), (0, 0), (0, 1)],
    [(3, 2), (2, 3), (3, 1), (1, 3)],
    [(0, 2), (0, 3), (3, 0), (3, 3)],
]
HIDDEN = [(-1, 0), (1, 0), (0, 1)]


def kernel(
    grid_x,
    grid_y,
    feat,
    heights,
    w_one,
    w_two,
    b_one,
    b_two,
    out,
    xx,
    stage,
    wall,
    bme,
    ball,
    bias,
    obuf,
    feat_sem,
    wl_sem,
    w_send,
    w_recv,
    b_send,
    b_recv,
    f_send,
    f_recv,
    h_send,
    h_recv,
    o_send,
    o_recv,
    o_local,
):
    column = lax.axis_index("space")
    chan = lax.axis_index("chan")
    core = chan % 2
    half = chan // 2
    col_x = column // grid_y
    col_y = column % grid_y
    fine_x = 2 * col_x + core
    fine_y = 2 * col_y + half
    depth = xx.shape[-1]
    base_y = 4 * half
    out_x = 2 * core - 1
    out_y = 2 * half - 1
    has_x = (col_x + out_x >= 0) & (col_x + out_x < grid_x)
    has_y = (col_y + out_y >= 0) & (col_y + out_y < grid_y)

    def device_at(a, b):
        fx, fy = fine_x + a * out_x, fine_y + b * out_y
        return ((fx // 2) * grid_y + fy // 2, (fy % 2) * 2 + fx % 2)

    def if_there(a, b):
        def run(action):
            if a == 1 and b == 1:
                pl.when(has_x & has_y)(action)
            elif a == 1:
                pl.when(has_x)(action)
            elif b == 1:
                pl.when(has_y)(action)
            else:
                action()

        return run

    def remote(src, dst, send_sem, recv_sem, target):
        return pltpu.make_async_remote_copy(
            src_ref=src,
            dst_ref=dst,
            send_sem=send_sem,
            recv_sem=recv_sem,
            device_id=target,
            device_id_type=MESH,
        )

    siblings = [
        (column, (1 - half) * 2 + core),
        (column, half * 2 + 1 - core),
        (column, (1 - half) * 2 + 1 - core),
    ]

    def feature_load(xl):
        return pltpu.make_async_copy(
            feat.at[0, :, 3 * core + xl], stage.at[xl], feat_sem.at[xl]
        )

    def turned(i):
        return 4 * core + (1 - 2 * core) * i

    for i in range(5):
        feature_load(turned(i)).start()
    weights = (w_one, w_two)

    def weight_load(layer):
        return pltpu.make_async_copy(
            weights[layer], wall.at[layer, chan], wl_sem.at[layer]
        )

    for layer in range(2):
        weight_load(layer).start()

    barrier = pltpu.get_barrier_semaphore()
    for a, b in PARTNERS:

        @if_there(a, b)
        def _():
            pl.semaphore_signal(
                barrier, inc=1, device_id=device_at(a, b), device_id_type=MESH
            )

    bme[...] = jnp.zeros_like(bme)
    bme[0:1, 0:32] = b_one[...]
    bme[1:2, 0:32] = b_two[...]
    ball[chan] = bme[...]

    live_top = heights[column] * 8
    lanes = lax.broadcasted_iota(jnp.int32, (1, 1, depth), 2)
    live_row = jnp.where(lanes < live_top, 1.0, 0.0).astype(jnp.bfloat16)

    def turn(i):
        xl = turned(i)
        feature_load(xl).wait()
        value = stage[xl] * live_row
        xx[0, xl + 1 - core, 1:9] = jnp.transpose(value, (1, 0, 2))

    def feature_send(a, b, i=None):
        src_x, dst_x = 1 + 3 * core, 5 - 5 * core
        src_y, dst_y = 1 + 7 * half, 9 - 9 * half
        if b == 0:
            run = pl.ds(1 + base_y, 4)
            src, dst = xx.at[0, src_x, run], xx.at[0, dst_x, run]
        else:
            run = pl.ds(1, 4) if i is None else turned(i) + 1 - core
            src, dst = xx.at[0, run, src_y], xx.at[0, run, dst_y]
        k = b
        return remote(src, dst, f_send.at[k], f_recv.at[k], device_at(a, b))

    FACES = ((1, 0), (0, 1))

    def passed_on(layer, k, send_sem, recv_sem):
        if k == 0:
            rows = pl.ds(3 + 2 * half, 2) if layer == 0 else 4 + half
            src = dst = xx.at[layer, 5 * core, rows]
        elif k == 1:
            src = xx.at[layer, 4 - 3 * core, 9 * half]
            dst = xx.at[layer, 5 * core, 9 * half]
        else:
            src = xx.at[layer, 5 * core, 1 + 7 * half]
            dst = xx.at[layer, 5 * core, 9 - 9 * half]
        return remote(src, dst, send_sem, recv_sem, device_at(0, 1) if k == 2 else siblings[k])

    def feature_pass(k):
        return passed_on(0, k, f_send.at[2 + k], f_recv.at[2 + k])

    def hidden_pass(k):
        return passed_on(1, k, h_send.at[3 + k], h_recv.at[3 + k])

    lax.fori_loop(0, 1, lambda i, carry: (turn(i), carry)[1], 0)

    def there(flag):
        return flag.astype(jnp.int32)

    pl.semaphore_wait(barrier, 3 + there(has_x) + there(has_y))

    def weight_send(layer, k):
        share = chan if k < 2 else siblings[0][1]
        src = weights[layer] if k < 2 else wall.at[layer, share]
        return remote(
            src,
            wall.at[layer, share],
            w_send.at[layer, k],
            w_recv.at[layer, k],
            siblings[0 if k == 0 else 1],
        )

    def bias_send(k):
        return remote(bme, ball.at[chan], b_send.at[k], b_recv.at[k], siblings[k])

    for k in range(2):
        weight_send(0, k).start()

    @if_there(1, 0)
    def _():
        feature_send(1, 0).start()

    for i in range(1):

        @if_there(0, 1)
        def _():
            feature_send(0, 1, i).start()

    for k in range(3):
        bias_send(k).start()

    def later_turn(i, carry):
        turn(i)

        @if_there(0, 1)
        def _():
            feature_send(0, 1, i).start()

        return carry

    lax.fori_loop(1, 4, later_turn, 0)
    turn(4)

    @pl.when(jnp.logical_not(has_x))
    def _():
        for layer in range(2):

            def clear(y, carry):
                xx[layer, 5 * core, y] = jnp.zeros((xx.shape[3], depth), xx.dtype)
                return carry

            lax.fori_loop(0, 10, clear, 0)

    @pl.when(jnp.logical_not(has_y))
    def _():
        for layer in range(2):

            def clear(x, carry):
                xx[layer, x, 9 * half] = jnp.zeros((xx.shape[3], depth), xx.dtype)
                return carry

            lax.fori_loop(0, 6, clear, 0)

    def relay(layer):
        weight_send(layer, 0).wait_recv()
        weight_send(layer, 2).start()

    relay(0)
    for k in range(2):
        weight_send(1, k).start()

    for k in range(3):
        bias_send(k).wait_recv()
    rows = lax.broadcasted_iota(jnp.int32, (32, 128), 0)
    cols = lax.broadcasted_iota(jnp.int32, (32, 128), 1)
    for layer in range(2):
        for c in range(4):
            spread = jnp.broadcast_to(ball[c, layer : layer + 1, :], (32, 128))
            column_of = jnp.sum(
                jnp.where(rows == cols, spread, 0.0), axis=1, keepdims=True
            )
            bias[layer, 32 * c : 32 * c + 32] = jnp.broadcast_to(column_of, (32, 128))

    def weights_ready(layer):
        weight_load(layer).wait()
        weight_send(layer, 1).wait_recv()
        weight_send(layer, 2).wait_recv()

    weights_ready(0)

    lane = lax.broadcasted_iota(jnp.int32, (128, depth), 1)

    def convolve(layer, px, py):
        rhs = jnp.concatenate(
            [xx[layer, px + i, base_y + py + j] for i in range(3) for j in range(3)],
            axis=0,
        )
        lhs = jnp.concatenate(
            [
                jnp.concatenate([wall[layer, c, 3 * t + k] for t in range(9)], axis=1)
                for k in range(3)
                for c in range(4)
            ],
            axis=0,
        )
        part = jnp.dot(lhs, rhs, preferred_element_type=jnp.float32)
        low = jnp.where(lane == 0, 0.0, pltpu.roll(part[0:128], 1, 1))
        high = jnp.where(lane == depth - 1, 0.0, pltpu.roll(part[256:384], depth - 1, 1))
        column_of = bias[layer]
        total = part[128:256] + low + high + jnp.concatenate([column_of] * (depth // 128), axis=1)
        total = jnp.where(lane < live_top, jnp.maximum(total, 0.0), 0.0)
        return total.astype(jnp.bfloat16)

    def listed(t, table):
        found = table[0]
        for k in range(1, len(table)):
            if table[k] != table[k - 1]:
                found = found + (table[k] - table[k - 1]) * lax.div(t + (8 - k), 8)
        return found

    def places(order, t):
        found = []
        for q in range(4):
            u = listed(t, [group[q][0] for group in order])
            v = listed(t, [group[q][1] for group in order])
            px = (1 - core) * 3 + out_x * u
            py = (1 - half) * 3 + out_y * v
            found.append((u, v, px, py))
        return found

    def at_edge(a, b, u, v):
        flag = None
        for side, value in ((a, u), (b, v)):
            if side != 0:
                mine = value == (3 if side == 1 else 0)
                flag = mine if flag is None else flag & mine
        return flag

    def hidden_send(a, b, px, py):
        src_x, src_y = px + 1, py + 1
        dst_x = src_x - 4 * a * out_x
        dst_y = src_y - 4 * b * out_y
        there_y = half if b == 0 else 1 - half
        k = HIDDEN.index((a, b))
        return remote(
            xx.at[1, src_x, base_y + src_y],
            xx.at[1, dst_x, 4 * there_y + dst_y],
            h_send.at[k],
            h_recv.at[k],
            device_at(a, b),
        )

    def hidden_whole(a, b, arrived):
        def edge(s, outer):
            if arrived:
                return 5 * outer if s == 1 else 5 - 5 * outer
            return 1 + 3 * (outer if s == 1 else 1 - outer)

        x = pl.ds(1, 4) if a == 0 else edge(a, core)
        if b != 0:
            y = base_y + edge(b, half)
        else:
            y = pl.ds(base_y + 1 - half, 5)
        k = HIDDEN.index((a, b))
        return remote(xx.at[1, x, y], xx.at[1, x, y], h_send.at[k], h_recv.at[k], device_at(a, b))

    def output_send(k, px=None, py=None):
        target = siblings[k]
        if px is None:
            src = obuf.at[target[1]]
            dst = out.at[pl.ds(4 * core, 4), pl.ds(4 * half, 4)]
        else:
            src = obuf.at[target[1], px, py]
            dst = out.at[4 * core + px, 4 * half + py]
        return remote(src, dst, o_send.at[k], o_recv.at[k], target)

    def first_step(t, carry):
        @pl.when(t == 3)
        def _():
            for k, (a, b) in enumerate(FACES):

                @if_there(a, b)
                def _():
                    feature_send(a, b).wait_recv()
                    feature_pass(k).start()

                if k == 0:

                    @if_there(1, 1)
                    def _():
                        feature_pass(2).start()

            relay(1)

        @pl.when(t == 4)
        def _():
            for k, (a, b) in enumerate(FACES):

                @if_there(a, b)
                def _():
                    feature_pass(k).wait_recv()

            @if_there(1, 1)
            def _():
                feature_pass(2).wait_recv()

        found = places(FIRST_ORDER, t)
        values = [convolve(0, px, py) for u, v, px, py in found]
        for (u, v, px, py), value in zip(found, values):
            xx[1, px + 1, base_y + py + 1] = value
        for u, v, px, py in found:
            for a, b in HIDDEN:

                @pl.when(at_edge(a, b, u, v))
                def _():
                    @if_there(a, b)
                    def _():
                        hidden_send(a, b, px, py).start()

        return carry

    lax.fori_loop(0, len(FIRST_ORDER), first_step, 0)

    weights_ready(1)

    def second_step(t, carry):
        @pl.when(t == 1)
        def _():
            hidden_whole(-1, 0, True).wait_recv()

        @pl.when(t == 2)
        def _():
            for k, (a, b) in enumerate(FACES):

                @if_there(a, b)
                def _():
                    hidden_whole(a, b, True).wait_recv()
                    if k == 1:
                        hidden_pass(1).start()

                if k == 0:

                    @if_there(1, 1)
                    def _():
                        hidden_pass(2).start()

        @pl.when(t == 3)
        def _():
            @if_there(0, 1)
            def _():
                hidden_pass(1).wait_recv()

            @if_there(1, 1)
            def _():
                hidden_pass(2).wait_recv()

        found = places(SECOND_ORDER, t)
        values = [convolve(1, px, py) for u, v, px, py in found]
        for (u, v, px, py), value in zip(found, values):
            for c in range(4):
                obuf[c, px, py] = value[32 * c : 32 * c + 32]
        for u, v, px, py in found:
            for k in (0, 2):
                output_send(k, px, py).start()

        return carry

    lax.fori_loop(0, len(SECOND_ORDER), second_step, 0)
    output_send(1).start()

    own = pltpu.make_async_copy(
        obuf.at[chan], out.at[pl.ds(4 * core, 4), pl.ds(4 * half, 4)], o_local
    )
    own.start()
    for k in range(3):
        bias_send(k).wait_send()
        for layer in range(2):
            weight_send(layer, k).wait_send()
    for a, b in FACES:

        @if_there(a, b)
        def _():
            feature_send(a, b).wait_send()

    for k, (a, b) in enumerate(FACES):

        @if_there(a, b)
        def _():
            feature_pass(k).wait_send()
            if k == 1:
                hidden_pass(1).wait_send()

    @if_there(1, 1)
    def _():
        feature_pass(2).wait_send()
        hidden_pass(2).wait_send()

    for a, b in HIDDEN:

        @if_there(a, b)
        def _():
            hidden_whole(a, b, False).wait_send()

    for k in range(3):
        output_send(k).wait_send()

    def arriving(k):
        target = siblings[k]
        there = (pl.ds(4 * (target[1] % 2), 4), pl.ds(4 * (target[1] // 2), 4))
        return remote(obuf.at[chan], out.at[there[0], there[1]], o_send.at[k], o_recv.at[k], target)

    for k in (1, 0, 2):
        arriving(k).wait_recv()
    own.wait()


def settle(gathered, out, held, turned, load_sems, store_sems):
    loads = [pltpu.make_async_copy(gathered.at[x], held.at[x], load_sems.at[x]) for x in range(8)]
    stores = [pltpu.make_async_copy(turned.at[x], out.at[0, :, x], store_sems.at[x]) for x in range(8)]
    for load in loads:
        load.start()
    for x in range(8):
        loads[x].wait()
        turned[x] = jnp.transpose(held[x], (1, 0, 2))
        stores[x].start()
    for store in stores:
        store.wait()


def on_device(features, column_heights, weight_one, bias_one, weight_two, bias_two):
    columns = lax.axis_size("space")
    depth = features.shape[4]
    bf16, f32 = jnp.bfloat16, jnp.float32
    anywhere = pl.BlockSpec(memory_space=pl.ANY)
    vmem = pl.BlockSpec(memory_space=pltpu.VMEM)
    smem = pl.BlockSpec(memory_space=pltpu.SMEM)
    dma = pltpu.SemaphoreType.DMA
    gathered = pl.pallas_call(
        functools.partial(kernel, columns // COL_Y, COL_Y),
        out_shape=jax.ShapeDtypeStruct((8, 8, 32, depth), bf16),
        in_specs=[anywhere, smem, anywhere, anywhere, vmem, vmem],
        out_specs=anywhere,
        scratch_shapes=[
            pltpu.VMEM((2, 6, 10, 128, depth), bf16),
            pltpu.VMEM((5, 128, 8, depth), bf16),
            pltpu.VMEM((2, 4, 27, 32, 128), bf16),
            pltpu.VMEM((8, 128), f32),
            pltpu.VMEM((4, 8, 128), f32),
            pltpu.VMEM((2, 128, 128), f32),
            pltpu.VMEM((4, 4, 4, 32, depth), bf16),
            dma((5,)),
            dma((2,)),
            dma((2, 3)),
            dma((2, 3)),
            dma((3,)),
            dma((3,)),
            dma((5,)),
            dma((5,)),
            dma((6,)),
            dma((6,)),
            dma((3,)),
            dma((3,)),
            dma,
        ],
        compiler_params=pltpu.CompilerParams(
            collective_id=0, has_side_effects=True, vmem_limit_bytes=60 << 20
        ),
        name="two_convolutions",
    )(
        features,
        column_heights,
        weight_one,
        weight_two,
        bias_one.reshape(1, 32),
        bias_two.reshape(1, 32),
    )
    return pl.pallas_call(
        settle,
        out_shape=jax.ShapeDtypeStruct((1, 32, 8, 8, depth), bf16),
        in_specs=[anywhere],
        out_specs=anywhere,
        scratch_shapes=[
            pltpu.VMEM((8, 8, 32, depth), bf16),
            pltpu.VMEM((8, 32, 8, depth), bf16),
            dma((8,)),
            dma((8,)),
        ],
        name="settle",
    )(gathered)


def solution(mesh):
    placed = (
        P("space", None, None, None, None),
        P(),
        P(None, "chan", None),
        P("chan"),
        P(None, "chan", None),
        P("chan"),
    )
    return jax.shard_map(
        on_device,
        mesh=mesh,
        in_specs=placed,
        out_specs=P("space", "chan", None, None, None),
        check_vma=False,
    )
```

```python
import functools

import jax
import jax.numpy as jnp
from jax import lax
from jax.experimental import pallas as pl
from jax.experimental.pallas import tpu as pltpu
from jax.sharding import PartitionSpec as P

COL_Y = 8
MESH = pl.DeviceIdType.MESH
PARTNERS = [(-1, 0), (0, -1), (-1, -1), (1, 0), (0, 1)]
FIRST_ORDER = [
    [(0, -1), (0, 0), (0, 1), (0, 2)],
    [(1, -1), (1, 0), (2, -1), (2, 0)],
    [(1, 1), (2, 1), (1, 2), (2, 2)],
    [(3, 1), (3, 2), (2, 3), (1, 3)],
    [(3, -1), (3, 0), (3, 3), (0, 3)],
]
SECOND_ORDER = [
    [(1, 0), (2, 0), (1, 1), (2, 1)],
    [(1, 2), (2, 2), (0, 0), (0, 1)],
    [(3, 2), (2, 3), (3, 1), (1, 3)],
    [(0, 2), (0, 3), (3, 0), (3, 3)],
]
HIDDEN = [(-1, 0), (1, 0), (0, 1)]


def kernel(
    grid_x,
    grid_y,
    feat,
    heights,
    w_one,
    w_two,
    b_one,
    b_two,
    out,
    xx,
    stage,
    wall,
    bme,
    ball,
    bias,
    obuf,
    feat_sem,
    wl_sem,
    w_send,
    w_recv,
    b_send,
    b_recv,
    f_send,
    f_recv,
    h_send,
    h_recv,
    o_send,
    o_recv,
    o_local,
):
    column = lax.axis_index("space")
    chan = lax.axis_index("chan")
    core = chan % 2
    half = chan // 2
    col_x = column // grid_y
    col_y = column % grid_y
    fine_x = 2 * col_x + core
    fine_y = 2 * col_y + half
    depth = xx.shape[-1]
    base_y = 4 * half
    out_x = 2 * core - 1
    out_y = 2 * half - 1
    has_x = (col_x + out_x >= 0) & (col_x + out_x < grid_x)
    has_y = (col_y + out_y >= 0) & (col_y + out_y < grid_y)

    def device_at(a, b):
        fx, fy = fine_x + a * out_x, fine_y + b * out_y
        return ((fx // 2) * grid_y + fy // 2, (fy % 2) * 2 + fx % 2)

    def if_there(a, b):
        def run(action):
            if a == 1 and b == 1:
                pl.when(has_x & has_y)(action)
            elif a == 1:
                pl.when(has_x)(action)
            elif b == 1:
                pl.when(has_y)(action)
            else:
                action()

        return run

    def remote(src, dst, send_sem, recv_sem, target):
        return pltpu.make_async_remote_copy(
            src_ref=src,
            dst_ref=dst,
            send_sem=send_sem,
            recv_sem=recv_sem,
            device_id=target,
            device_id_type=MESH,
        )

    siblings = [
        (column, (1 - half) * 2 + core),
        (column, half * 2 + 1 - core),
        (column, (1 - half) * 2 + 1 - core),
    ]

    barrier = pltpu.get_barrier_semaphore()
    for a, b in PARTNERS:

        @if_there(a, b)
        def _():
            pl.semaphore_signal(
                barrier, inc=1, device_id=device_at(a, b), device_id_type=MESH
            )

    def feature_load(xl):
        return pltpu.make_async_copy(
            feat.at[0, :, 3 * core + xl], stage.at[xl], feat_sem.at[xl]
        )

    def turned(i):
        return 4 * core + (1 - 2 * core) * i

    for i in range(5):
        feature_load(turned(i)).start()
    weights = (w_one, w_two)

    def weight_load(layer):
        return pltpu.make_async_copy(
            weights[layer], wall.at[layer, chan], wl_sem.at[layer]
        )

    for layer in range(2):
        weight_load(layer).start()

    bme[...] = jnp.zeros_like(bme)
    bme[0:1, 0:32] = b_one[...]
    bme[1:2, 0:32] = b_two[...]
    ball[chan] = bme[...]

    live_top = heights[column] * 8
    lanes = lax.broadcasted_iota(jnp.int32, (1, 1, depth), 2)
    live_row = jnp.where(lanes < live_top, 1.0, 0.0).astype(jnp.bfloat16)

    def turn(i):
        xl = turned(i)
        feature_load(xl).wait()
        value = stage[xl] * live_row
        xx[0, xl + 1 - core, 1:9] = jnp.transpose(value, (1, 0, 2))

    def feature_send(a, b, i=None):
        src_x, dst_x = 1 + 3 * core, 5 - 5 * core
        src_y, dst_y = 1 + 7 * half, 9 - 9 * half
        if b == 0:
            run = pl.ds(1 + base_y, 4)
            src, dst = xx.at[0, src_x, run], xx.at[0, dst_x, run]
        else:
            run = pl.ds(1, 4) if i is None else turned(i) + 1 - core
            src, dst = xx.at[0, run, src_y], xx.at[0, run, dst_y]
        k = b
        return remote(src, dst, f_send.at[k], f_recv.at[k], device_at(a, b))

    FACES = ((1, 0), (0, 1))

    def passed_on(layer, k, send_sem, recv_sem):
        if k == 0:
            rows = pl.ds(3 + 2 * half, 2) if layer == 0 else 4 + half
            src = dst = xx.at[layer, 5 * core, rows]
        elif k == 1:
            src = xx.at[layer, 4 - 3 * core, 9 * half]
            dst = xx.at[layer, 5 * core, 9 * half]
        else:
            src = xx.at[layer, 5 * core, 1 + 7 * half]
            dst = xx.at[layer, 5 * core, 9 - 9 * half]
        return remote(src, dst, send_sem, recv_sem, device_at(0, 1) if k == 2 else siblings[k])

    def feature_pass(k):
        return passed_on(0, k, f_send.at[2 + k], f_recv.at[2 + k])

    def hidden_pass(k):
        return passed_on(1, k, h_send.at[3 + k], h_recv.at[3 + k])

    lax.fori_loop(0, 1, lambda i, carry: (turn(i), carry)[1], 0)

    def there(flag):
        return flag.astype(jnp.int32)

    pl.semaphore_wait(barrier, 3 + there(has_x) + there(has_y))

    def weight_send(layer, k):
        share = chan if k < 2 else siblings[0][1]
        src = weights[layer] if k < 2 else wall.at[layer, share]
        return remote(
            src,
            wall.at[layer, share],
            w_send.at[layer, k],
            w_recv.at[layer, k],
            siblings[0 if k == 0 else 1],
        )

    def bias_send(k):
        return remote(bme, ball.at[chan], b_send.at[k], b_recv.at[k], siblings[k])

    for k in range(2):
        weight_send(0, k).start()

    @if_there(1, 0)
    def _():
        feature_send(1, 0).start()

    for i in range(1):

        @if_there(0, 1)
        def _():
            feature_send(0, 1, i).start()

    for k in range(3):
        bias_send(k).start()

    def later_turn(i, carry):
        turn(i)

        @if_there(0, 1)
        def _():
            feature_send(0, 1, i).start()

        return carry

    lax.fori_loop(1, 4, later_turn, 0)
    turn(4)

    @pl.when(jnp.logical_not(has_x))
    def _():
        for layer in range(2):

            def clear(y, carry):
                xx[layer, 5 * core, y] = jnp.zeros((xx.shape[3], depth), xx.dtype)
                return carry

            lax.fori_loop(0, 10, clear, 0)

    @pl.when(jnp.logical_not(has_y))
    def _():
        for layer in range(2):

            def clear(x, carry):
                xx[layer, x, 9 * half] = jnp.zeros((xx.shape[3], depth), xx.dtype)
                return carry

            lax.fori_loop(0, 6, clear, 0)

    def relay(layer):
        weight_send(layer, 0).wait_recv()
        weight_send(layer, 2).start()

    relay(0)
    for k in range(2):
        weight_send(1, k).start()

    for k in range(3):
        bias_send(k).wait_recv()
    rows = lax.broadcasted_iota(jnp.int32, (32, 128), 0)
    cols = lax.broadcasted_iota(jnp.int32, (32, 128), 1)
    for layer in range(2):
        for c in range(4):
            spread = jnp.broadcast_to(ball[c, layer : layer + 1, :], (32, 128))
            column_of = jnp.sum(
                jnp.where(rows == cols, spread, 0.0), axis=1, keepdims=True
            )
            bias[layer, 32 * c : 32 * c + 32] = jnp.broadcast_to(column_of, (32, 128))

    def weights_ready(layer):
        weight_load(layer).wait()
        weight_send(layer, 1).wait_recv()
        weight_send(layer, 2).wait_recv()

    weights_ready(0)

    lane = lax.broadcasted_iota(jnp.int32, (128, depth), 1)

    def convolve(layer, px, py):
        rhs = jnp.concatenate(
            [xx[layer, px + i, base_y + py + j] for i in range(3) for j in range(3)],
            axis=0,
        )
        lhs = jnp.concatenate(
            [
                jnp.concatenate([wall[layer, c, 3 * t + k] for t in range(9)], axis=1)
                for k in range(3)
                for c in range(4)
            ],
            axis=0,
        )
        part = jnp.dot(lhs, rhs, preferred_element_type=jnp.float32)
        low = jnp.where(lane == 0, 0.0, pltpu.roll(part[0:128], 1, 1))
        high = jnp.where(lane == depth - 1, 0.0, pltpu.roll(part[256:384], depth - 1, 1))
        column_of = bias[layer]
        total = part[128:256] + low + high + jnp.concatenate([column_of] * (depth // 128), axis=1)
        total = jnp.where(lane < live_top, jnp.maximum(total, 0.0), 0.0)
        return total.astype(jnp.bfloat16)

    def listed(t, table):
        found = table[0]
        for k in range(1, len(table)):
            if table[k] != table[k - 1]:
                found = found + (table[k] - table[k - 1]) * lax.div(t + (8 - k), 8)
        return found

    def places(order, t):
        found = []
        for q in range(4):
            u = listed(t, [group[q][0] for group in order])
            v = listed(t, [group[q][1] for group in order])
            px = (1 - core) * 3 + out_x * u
            py = (1 - half) * 3 + out_y * v
            found.append((u, v, px, py))
        return found

    def at_edge(a, b, u, v):
        flag = None
        for side, value in ((a, u), (b, v)):
            if side != 0:
                mine = value == (3 if side == 1 else 0)
                flag = mine if flag is None else flag & mine
        return flag

    def hidden_send(a, b, px, py):
        src_x, src_y = px + 1, py + 1
        dst_x = src_x - 4 * a * out_x
        dst_y = src_y - 4 * b * out_y
        there_y = half if b == 0 else 1 - half
        k = HIDDEN.index((a, b))
        return remote(
            xx.at[1, src_x, base_y + src_y],
            xx.at[1, dst_x, 4 * there_y + dst_y],
            h_send.at[k],
            h_recv.at[k],
            device_at(a, b),
        )

    def hidden_whole(a, b, arrived):
        def edge(s, outer):
            if arrived:
                return 5 * outer if s == 1 else 5 - 5 * outer
            return 1 + 3 * (outer if s == 1 else 1 - outer)

        x = pl.ds(1, 4) if a == 0 else edge(a, core)
        if b != 0:
            y = base_y + edge(b, half)
        else:
            y = pl.ds(base_y + 1 - half, 5)
        k = HIDDEN.index((a, b))
        return remote(xx.at[1, x, y], xx.at[1, x, y], h_send.at[k], h_recv.at[k], device_at(a, b))

    def output_send(k, px=None, py=None):
        target = siblings[k]
        if px is None:
            src = obuf.at[target[1]]
            dst = out.at[pl.ds(4 * core, 4), pl.ds(4 * half, 4)]
        else:
            src = obuf.at[target[1], px, py]
            dst = out.at[4 * core + px, 4 * half + py]
        return remote(src, dst, o_send.at[k], o_recv.at[k], target)

    def first_step(t, carry):
        @pl.when(t == 3)
        def _():
            for k, (a, b) in enumerate(FACES):

                @if_there(a, b)
                def _():
                    feature_send(a, b).wait_recv()
                    feature_pass(k).start()

                if k == 0:

                    @if_there(1, 1)
                    def _():
                        feature_pass(2).start()

            relay(1)

        @pl.when(t == 4)
        def _():
            for k, (a, b) in enumerate(FACES):

                @if_there(a, b)
                def _():
                    feature_pass(k).wait_recv()

            @if_there(1, 1)
            def _():
                feature_pass(2).wait_recv()

        found = places(FIRST_ORDER, t)
        values = [convolve(0, px, py) for u, v, px, py in found]
        for (u, v, px, py), value in zip(found, values):
            xx[1, px + 1, base_y + py + 1] = value
        for u, v, px, py in found:
            for a, b in HIDDEN:

                @pl.when(at_edge(a, b, u, v))
                def _():
                    @if_there(a, b)
                    def _():
                        hidden_send(a, b, px, py).start()

        return carry

    lax.fori_loop(0, len(FIRST_ORDER), first_step, 0)

    weights_ready(1)

    def second_step(t, carry):
        @pl.when(t == 1)
        def _():
            hidden_whole(-1, 0, True).wait_recv()

        @pl.when(t == 2)
        def _():
            for k, (a, b) in enumerate(FACES):

                @if_there(a, b)
                def _():
                    hidden_whole(a, b, True).wait_recv()
                    if k == 1:
                        hidden_pass(1).start()

                if k == 0:

                    @if_there(1, 1)
                    def _():
                        hidden_pass(2).start()

        @pl.when(t == 3)
        def _():
            @if_there(0, 1)
            def _():
                hidden_pass(1).wait_recv()

            @if_there(1, 1)
            def _():
                hidden_pass(2).wait_recv()

        found = places(SECOND_ORDER, t)
        values = [convolve(1, px, py) for u, v, px, py in found]
        for (u, v, px, py), value in zip(found, values):
            for c in range(4):
                obuf[c, px, py] = value[32 * c : 32 * c + 32]
        for u, v, px, py in found:
            for k in (0, 2):
                output_send(k, px, py).start()

        return carry

    lax.fori_loop(0, len(SECOND_ORDER), second_step, 0)
    output_send(1).start()

    own = pltpu.make_async_copy(
        obuf.at[chan], out.at[pl.ds(4 * core, 4), pl.ds(4 * half, 4)], o_local
    )
    own.start()
    for k in range(3):
        bias_send(k).wait_send()
        for layer in range(2):
            weight_send(layer, k).wait_send()
    for a, b in FACES:

        @if_there(a, b)
        def _():
            feature_send(a, b).wait_send()

    for k, (a, b) in enumerate(FACES):

        @if_there(a, b)
        def _():
            feature_pass(k).wait_send()
            if k == 1:
                hidden_pass(1).wait_send()

    @if_there(1, 1)
    def _():
        feature_pass(2).wait_send()
        hidden_pass(2).wait_send()

    for a, b in HIDDEN:

        @if_there(a, b)
        def _():
            hidden_whole(a, b, False).wait_send()

    for k in range(3):
        output_send(k).wait_send()

    def arriving(k):
        target = siblings[k]
        there = (pl.ds(4 * (target[1] % 2), 4), pl.ds(4 * (target[1] // 2), 4))
        return remote(obuf.at[chan], out.at[there[0], there[1]], o_send.at[k], o_recv.at[k], target)

    for k in (1, 0, 2):
        arriving(k).wait_recv()
    own.wait()


def settle(gathered, out, held, turned, load_sems, store_sems):
    loads = [pltpu.make_async_copy(gathered.at[x], held.at[x], load_sems.at[x]) for x in range(8)]
    stores = [pltpu.make_async_copy(turned.at[x], out.at[0, :, x], store_sems.at[x]) for x in range(8)]
    for load in loads:
        load.start()
    for x in range(8):
        loads[x].wait()
        turned[x] = jnp.transpose(held[x], (1, 0, 2))
        stores[x].start()
    for store in stores:
        store.wait()


def on_device(features, column_heights, weight_one, bias_one, weight_two, bias_two):
    columns = lax.axis_size("space")
    depth = features.shape[4]
    bf16, f32 = jnp.bfloat16, jnp.float32
    anywhere = pl.BlockSpec(memory_space=pl.ANY)
    vmem = pl.BlockSpec(memory_space=pltpu.VMEM)
    smem = pl.BlockSpec(memory_space=pltpu.SMEM)
    dma = pltpu.SemaphoreType.DMA
    gathered = pl.pallas_call(
        functools.partial(kernel, columns // COL_Y, COL_Y),
        out_shape=jax.ShapeDtypeStruct((8, 8, 32, depth), bf16),
        in_specs=[anywhere, smem, anywhere, anywhere, vmem, vmem],
        out_specs=anywhere,
        scratch_shapes=[
            pltpu.VMEM((2, 6, 10, 128, depth), bf16),
            pltpu.VMEM((5, 128, 8, depth), bf16),
            pltpu.VMEM((2, 4, 27, 32, 128), bf16),
            pltpu.VMEM((8, 128), f32),
            pltpu.VMEM((4, 8, 128), f32),
            pltpu.VMEM((2, 128, 128), f32),
            pltpu.VMEM((4, 4, 4, 32, depth), bf16),
            dma((5,)),
            dma((2,)),
            dma((2, 3)),
            dma((2, 3)),
            dma((3,)),
            dma((3,)),
            dma((5,)),
            dma((5,)),
            dma((6,)),
            dma((6,)),
            dma((3,)),
            dma((3,)),
            dma,
        ],
        compiler_params=pltpu.CompilerParams(
            collective_id=0, has_side_effects=True, vmem_limit_bytes=60 << 20
        ),
        name="two_convolutions",
    )(
        features,
        column_heights,
        weight_one,
        weight_two,
        bias_one.reshape(1, 32),
        bias_two.reshape(1, 32),
    )
    return pl.pallas_call(
        settle,
        out_shape=jax.ShapeDtypeStruct((1, 32, 8, 8, depth), bf16),
        in_specs=[anywhere],
        out_specs=anywhere,
        scratch_shapes=[
            pltpu.VMEM((8, 8, 32, depth), bf16),
            pltpu.VMEM((8, 32, 8, depth), bf16),
            dma((8,)),
            dma((8,)),
        ],
        name="settle",
    )(gathered)


def solution(mesh):
    placed = (
        P("space", None, None, None, None),
        P(),
        P(None, "chan", None),
        P("chan"),
        P(None, "chan", None),
        P("chan"),
    )
    return jax.shard_map(
        on_device,
        mesh=mesh,
        in_specs=placed,
        out_specs=P("space", "chan", None, None, None),
        check_vma=False,
    )
```
